256 devices in a mesh: len: 32 (over z, y), wid: 8 (over x, core).
Axes of the slice: x: 4, y: 4, z: 8, core: 2. Of those that a mesh axis runs over, the one named last changes fastest.
Arguments:
- positions: float32 [32, 8, 192, 3, 128], P('len', 'wid'), may hold values from 0 to 8
- velocities: float32 [32, 8, 192, 3, 128], P('len', 'wid'), may hold values from -4 to 4
- spins: float32 [32, 8, 192, 3, 128], P('len', 'wid'), may hold values from -4 to 4
- sphere_radii: float32 [32, 8, 192, 128], P('len', 'wid'), may hold values from 0.4 to 0.6
- swap_counts: int32 [32, 8, 8], P('len', 'wid'), may hold values from 0 to 24, as said below
- swap_slots: int32 [32, 8, 8, 24], P('len', 'wid'), may hold values from 0 to 191, as said below
- ghost_slots: int32 [32, 8, 4, 48], P('len', 'wid'), may hold values from 0 to 191, as said below
- corner_slots: int32 [32, 8, 4, 4], P('len', 'wid'), may hold values from 0 to 191, as said below
- pair_first: int32 [32, 8, 128], P('len', 'wid'), may hold values from 0 to 191
- pair_second: int32 [32, 8, 128], P('len', 'wid'), may hold values from 0 to 399, as said below
- pair_live: int32 [32, 8], P('len', 'wid'), may hold values from 1 to 128, as said below
Outputs:
- positions_out: float32 [32, 8, 192, 3, 128], P('len', 'wid')
- velocities_out: float32 [32, 8, 192, 3, 128], P('len', 'wid')
- spins_out: float32 [32, 8, 192, 3, 128], P('len', 'wid')
- sphere_radii_out: float32 [32, 8, 192, 128], P('len', 'wid')
The draws below stay inside these ranges and needn't reach their ends.
Inputs may be any that keep to these rules, and one draw needn't show every extreme that they name: `swap_counts`: equal on the two partners of each step; some pair exchanges 24 blocks in every step. `swap_slots`: distinct within one device and step. `ghost_slots`: distinct within one device and direction. `corner_slots`: distinct within one device and direction. `pair_second`: never names a ghost block from a neighbour outside the grid. Only the first pair_live entries of a device's lists are used; some device uses all 128.
All inputs are finite; a program needn't handle non-finite values.
Results may differ from the reference program's by a relative error of at most 0.0003.
Values sent between devices are 32-bit elements; how exact they have to be, the bound alone decides.
No kernel may reach another device: no remote copies, remote signals or barrier semaphores. Data moves between devices by JAX's collectives and lax.ppermute only.
A program may use at most 64 MiB of HBM per device.

```python
import math
import jax
import jax.numpy as jnp
from jax import lax

BLK = 128
S = 192
MOVE = 24
GHOST = 48
CORNER = 4
EXT = 400
PAIRS = 128
LBITS = 5
BITS = 8
N_LEN = 32
N_WID = 8


def draw_swap_counts(key, part):
    drawn = jax.random.randint(jax.random.fold_in(key, 11), (N_LEN, N_WID, BITS), 0, MOVE + 1)
    length_index = jnp.arange(N_LEN, dtype=jnp.int32)[:, None, None]
    width_index = jnp.arange(N_WID, dtype=jnp.int32)[None, :, None]
    levels = jnp.arange(BITS, dtype=jnp.int32)[None, None, :]
    len_mask = jnp.where(levels < LBITS, jnp.left_shift(1, jnp.minimum(levels, LBITS - 1)), 0)
    wid_mask = jnp.where(levels >= LBITS, jnp.left_shift(1, jnp.maximum(levels - LBITS, 0)), 0)
    low_length = length_index - jnp.bitwise_and(length_index, len_mask)
    low_width = width_index - jnp.bitwise_and(width_index, wid_mask)
    counts = drawn[low_length, low_width, levels]
    full_length = jax.random.randint(jax.random.fold_in(key, 12), (), 0, N_LEN)
    full_width = jax.random.randint(jax.random.fold_in(key, 13), (), 0, N_WID)
    empty_length = (full_length + N_LEN // 2) % N_LEN
    empty_width = (full_width + N_WID // 2) % N_WID
    is_full = (low_length == full_length - jnp.bitwise_and(full_length, len_mask)) & (low_width == full_width - jnp.bitwise_and(full_width, wid_mask))
    is_empty = (low_length == empty_length - jnp.bitwise_and(empty_length, len_mask)) & (low_width == empty_width - jnp.bitwise_and(empty_width, wid_mask))
    counts = jnp.where(is_full, MOVE, jnp.where(is_empty, 0, counts))
    return counts.astype(jnp.int32)


def draw_swap_slots(key, part):
    scores = jax.random.randint(jax.random.fold_in(key, 21), (N_LEN, N_WID, BITS, S), 0, 1 << 20) * S + jnp.arange(S, dtype=jnp.int32)
    return jnp.argsort(scores, axis=-1)[..., :MOVE].astype(jnp.int32)


def draw_ghost_slots(key, part):
    scores = jax.random.randint(jax.random.fold_in(key, 31), (N_LEN, N_WID, 4, S), 0, 1 << 20) * S + jnp.arange(S, dtype=jnp.int32)
    return jnp.argsort(scores, axis=-1)[..., :GHOST].astype(jnp.int32)


def draw_corner_slots(key, part):
    scores = jax.random.randint(jax.random.fold_in(key, 35), (N_LEN, N_WID, 4, S), 0, 1 << 20) * S + jnp.arange(S, dtype=jnp.int32)
    return jnp.argsort(scores, axis=-1)[..., :CORNER].astype(jnp.int32)


def draw_pair_second(key, part):
    drawn = jax.random.randint(jax.random.fold_in(key, 41), (N_LEN, N_WID, PAIRS), 0, EXT)
    drawn = drawn.at[1, 1, 0].set(EXT - 1)
    length_index = jnp.arange(N_LEN, dtype=jnp.int32)[:, None, None]
    width_index = jnp.arange(N_WID, dtype=jnp.int32)[None, :, None]
    face_dir = jnp.clip((drawn - S) // GHOST, 0, 3)
    corner_dir = 4 + jnp.clip((drawn - S - 4 * GHOST) // CORNER, 0, 3)
    direction = jnp.where(drawn < S + 4 * GHOST, face_dir, corner_dir)
    length_steps = jnp.array([-1, 0, 0, 1, -1, -1, 1, 1], dtype=jnp.int32)[direction]
    width_steps = jnp.array([0, -1, 1, 0, -1, 1, -1, 1], dtype=jnp.int32)[direction]
    source_length = length_index - length_steps
    source_width = width_index - width_steps
    inside = (source_length >= 0) & (source_length < N_LEN) & (source_width >= 0) & (source_width < N_WID)
    return jnp.where((drawn < S) | inside, drawn, drawn % S).astype(jnp.int32)


def draw_pair_live(key, part):
    left_draw = jax.random.randint(jax.random.fold_in(key, 51), (N_LEN, N_WID), 0, PAIRS)
    right_draw = jax.random.randint(jax.random.fold_in(key, 52), (N_LEN, N_WID), 0, PAIRS)
    live_count = 1 + jnp.minimum(left_draw, right_draw)
    full_length = jax.random.randint(jax.random.fold_in(key, 53), (), 0, N_LEN)
    full_width = jax.random.randint(jax.random.fold_in(key, 54), (), 0, N_WID)
    live_count = live_count.at[full_length, full_width].set(PAIRS)
    live_count = live_count.at[(full_length + N_LEN // 2) % N_LEN, full_width].set(1)
    return live_count.astype(jnp.int32)


def touch_ends(result, rng, least, largest):
    index_at = [jax.random.randint(jax.random.fold_in(rng, axis), (), 0, length) for axis, length in enumerate(result.shape)]
    longest = result.shape.index(max(result.shape))
    beside = index_at[:longest] + [(index_at[longest] + 1) % result.shape[longest]] + index_at[longest + 1:]
    return result.at[tuple(index_at)].set(least).at[tuple(beside)].set(largest)


def steps_of(own_key, extent, split, low, top_value):
    gain = 1.0
    for position, shards_of in split:
        draws = jax.random.uniform(jax.random.fold_in(jax.random.fold_in(own_key, 6), position), (shards_of,), jnp.float32, low / len(split), top_value / len(split))
        gain = gain * jnp.repeat(jnp.exp(draws), extent[position] // shards_of).reshape((-1,) + (1,) * (len(extent) - 1 - position))
    return gain


def bell_draw(rng, extent, width, bound, cuts=(), kind=jnp.bfloat16):
    values = width * jax.random.normal(rng, extent, jnp.float32)
    if cuts:
        values = values * steps_of(rng, extent, cuts, -0.22, 0.18)
    return jnp.clip(values, -bound, bound).astype(kind)


def setup_inputs(seed: int = 0) -> dict:
    keys = jax.random.split(jax.random.key(seed), 12)
    positions = jnp.clip(8.0 * jax.random.uniform(keys[0], (N_LEN, N_WID, S, 3, BLK), jnp.float32) ** steps_of(keys[0], (N_LEN, N_WID, S, 3, BLK), ((0, 32), (1, 8)), -0.2, 0.2), 0.0, 8.0)
    velocities = bell_draw(keys[1], (N_LEN, N_WID, S, 3, BLK), 1.0, 4.0, ((0, 32), (1, 8)), jnp.float32)
    spins = bell_draw(keys[2], (N_LEN, N_WID, S, 3, BLK), 1.0, 4.0, ((0, 32), (1, 8)), jnp.float32)
    sphere_radii = jnp.clip(0.4 + 0.20000002 * jax.random.uniform(keys[3], (N_LEN, N_WID, S, BLK), jnp.float32) ** steps_of(keys[3], (N_LEN, N_WID, S, BLK), ((0, 32), (1, 8)), -0.2, 0.2), 0.4, 0.6)
    swap_counts = draw_swap_counts(jax.random.fold_in(keys[11], 71), 0)
    swap_slots = draw_swap_slots(jax.random.fold_in(keys[11], 71), 0)
    ghost_slots = draw_ghost_slots(jax.random.fold_in(keys[11], 71), 0)
    corner_slots = draw_corner_slots(jax.random.fold_in(keys[11], 71), 0)
    pair_first = touch_ends(jax.random.randint(keys[8], (N_LEN, N_WID, PAIRS), 0, S), jax.random.fold_in(keys[8], 1), 0, S - 1).astype(jnp.int32)
    pair_second = draw_pair_second(jax.random.fold_in(keys[11], 71), 0)
    pair_live = draw_pair_live(jax.random.fold_in(keys[11], 71), 0)
    return dict(positions=positions, velocities=velocities, spins=spins, sphere_radii=sphere_radii, swap_counts=swap_counts, swap_slots=swap_slots, ghost_slots=ghost_slots, corner_slots=corner_slots, pair_first=pair_first, pair_second=pair_second, pair_live=pair_live)


SOFTENING = 0.1
STIFFNESS = 600.0
DAMPING = 20.0
FRICTION = 0.5
SLIP_SPEED = 0.1
DENSITY = 1.9
TIME_STEP = 0.01
DIRECTIONS = ((-1, 0), (0, -1), (0, 1), (1, 0), (-1, -1), (-1, 1), (1, -1), (1, 1))

def cross_product(left_vector, right_vector):
    return jnp.stack([left_vector[:, 1] * right_vector[:, 2] - left_vector[:, 2] * right_vector[:, 1], left_vector[:, 2] * right_vector[:, 0] - left_vector[:, 0] * right_vector[:, 2], left_vector[:, 0] * right_vector[:, 1] - left_vector[:, 1] * right_vector[:, 0]], axis=1)

def contact(near_block, far_block):
    near_position = near_block[:, 0:3, :, None]
    near_velocity = near_block[:, 3:6, :, None]
    near_spin = near_block[:, 6:9, :, None]
    near_radius = near_block[:, 9, :, None]
    far_position = far_block[:, 0:3, None, :]
    far_velocity = far_block[:, 3:6, None, :]
    far_spin = far_block[:, 6:9, None, :]
    far_radius = far_block[:, 9, None, :]
    offset = far_position - near_position
    distance = jnp.sqrt(lax.optimization_barrier(jnp.sum(offset * offset, axis=1)) + SOFTENING * SOFTENING)
    normal = offset / distance[:, None]
    indent = jnp.maximum(near_radius + far_radius - distance, 0.0)
    root_depth = jnp.sqrt(indent)
    lever_arm = near_radius[:, None] * near_spin + far_radius[:, None] * far_spin
    relative = far_velocity - near_velocity - cross_product(lever_arm, normal)
    approach = lax.optimization_barrier(jnp.sum(relative * normal, axis=1))
    normal_force = jnp.maximum(STIFFNESS * indent * root_depth - DAMPING * root_depth * approach, 0.0)
    tangent = relative - approach[:, None] * normal
    slip_norm = jnp.sqrt(lax.optimization_barrier(jnp.sum(tangent * tangent, axis=1)) + SLIP_SPEED * SLIP_SPEED)
    friction_force = (FRICTION * normal_force / slip_norm)[:, None] * tangent
    total_force = lax.optimization_barrier(jnp.sum(friction_force - normal_force[:, None] * normal, axis=3))
    torque = near_block[:, 9][:, None] * lax.optimization_barrier(jnp.sum(cross_product(normal, friction_force), axis=3))
    return jnp.concatenate([total_force, torque], axis=1)

def place_blocks(blocks, partner_blocks, own_slots, partner_slots, count):
    incoming = partner_blocks[partner_slots]
    current = blocks[own_slots]
    keep = jnp.arange(own_slots.shape[0], dtype=jnp.int32) < count
    return blocks.at[own_slots].set(jnp.where(keep[:, None, None], incoming, current))

def pick_rows(blocks, rows):
    return blocks[rows]

def device_forces(inputs):
    owned, extended, first_list, second_list, live_count = inputs

    def group_forces(totals, group_start):
        entries = group_start + jnp.arange(16, dtype=jnp.int32)
        terms = contact(owned[first_list[entries]], extended[second_list[entries]])
        weight = (entries < live_count).astype(terms.dtype)
        added = jax.ops.segment_sum(terms * weight[:, None, None], first_list[entries], num_segments=S)
        return (totals + added, None)
    group_starts = jnp.arange(0, PAIRS, 16, dtype=jnp.int32)
    totals, _ = lax.scan(group_forces, jnp.zeros((S, 6, BLK), jnp.float32), group_starts)
    return totals

def reference(positions, velocities, spins, sphere_radii, swap_counts, swap_slots, ghost_slots, corner_slots, pair_first, pair_second, pair_live):
    packed = jnp.concatenate([positions, velocities, spins, sphere_radii[:, :, :, None, :]], axis=3)
    length_index = jnp.arange(N_LEN, dtype=jnp.int32)
    width_index = jnp.arange(N_WID, dtype=jnp.int32)
    placer = jax.vmap(jax.vmap(place_blocks))
    for level in range(BITS):
        if level < LBITS:
            partner = jnp.bitwise_xor(length_index, 1 << level)
            partner_state = packed[partner]
            partner_slots = swap_slots[partner]
        else:
            partner = jnp.bitwise_xor(width_index, 1 << level - LBITS)
            partner_state = packed[:, partner]
            partner_slots = swap_slots[:, partner]
        packed = placer(packed, partner_state, swap_slots[:, :, level], partner_slots[:, :, level], swap_counts[:, :, level])
    face_out = jax.vmap(jax.vmap(pick_rows))(packed, ghost_slots)
    corner_out = jax.vmap(jax.vmap(pick_rows))(packed, corner_slots)
    pieces = []
    for direction, (length_step, across) in enumerate(DIRECTIONS):
        if direction < 4:
            source = face_out[:, :, direction]
        else:
            source = corner_out[:, :, direction - 4]
        padded = jnp.pad(source, ((1, 1), (1, 1), (0, 0), (0, 0), (0, 0)))
        pieces.append(padded[1 - length_step:1 - length_step + N_LEN, 1 - across:1 - across + N_WID])
    extended = jnp.concatenate([packed] + pieces, axis=2)
    totals = lax.map(device_forces, (packed.reshape(N_LEN * N_WID, S, 10, BLK), extended.reshape(N_LEN * N_WID, EXT, 10, BLK), pair_first.reshape(N_LEN * N_WID, PAIRS), pair_second.reshape(N_LEN * N_WID, PAIRS), pair_live.reshape(N_LEN * N_WID)))
    totals = totals.reshape(N_LEN, N_WID, S, 6, BLK)
    radius_now = packed[:, :, :, 9, :]
    masses = DENSITY * (4.0 / 3.0) * math.pi * radius_now * radius_now * radius_now
    inertia = 0.4 * masses * radius_now * radius_now
    velocities_out = packed[:, :, :, 3:6, :] + TIME_STEP * totals[:, :, :, 0:3, :] / masses[:, :, :, None, :]
    spins_out = packed[:, :, :, 6:9, :] + TIME_STEP * totals[:, :, :, 3:6, :] / inertia[:, :, :, None, :]
    positions_out = packed[:, :, :, 0:3, :] + TIME_STEP * velocities_out
    return (positions_out, velocities_out, spins_out, radius_now)
```

```python
import functools
import math

import jax
import jax.numpy as jnp
from jax import lax
from jax.experimental import pallas as pl
from jax.experimental.pallas import tpu as pltpu
from jax.sharding import PartitionSpec as P

DENSITY = 1.9
TIME_STEP = 0.01
BLK = 128
S = 192
MOVE = 24
GHOST = 48
CORNER = 4
PAIRS = 128
BITS = 8
LBITS = 5
ROWS = 10
OWN = S
RECV = MOVE * BITS
WIDE = GHOST + 2 * CORNER
G_WA, G_WB, G_LA, G_LB = 0, GHOST, 2 * GHOST, 2 * GHOST + WIDE
GHOSTS = 2 * GHOST + 2 * WIDE
GBASE = OWN + RECV
T_SEND, T_FINAL, T_GHOST, T_CORNER = 0, 192, 384, 576
T_SIZE = 640
Q_A, Q_B, Q_SLOT, Q_END = 0, 128, 256, 384
Q_SIZE = 512
FIRST_WINDOW = 2
CAP = 9
CAP_ROWS = 16
CATS = 11

SMEM = pl.BlockSpec(memory_space=pltpu.SMEM)
VMEM = pl.BlockSpec(memory_space=pltpu.VMEM)
ANY = pl.BlockSpec(memory_space=pl.ANY)


def f32(*shape):
    return jax.ShapeDtypeStruct(shape, jnp.float32)


def vmem(*shape):
    return pltpu.VMEM(shape, jnp.float32)


def call(body, out_shape, in_specs, out_specs, scratch=(), name=None, flops=0):
    return pl.pallas_call(
        body,
        out_shape=out_shape,
        in_specs=in_specs,
        out_specs=out_specs,
        scratch_shapes=list(scratch),
        name=name,
        compiler_params=pltpu.CompilerParams(vmem_limit_bytes=24 * 1024 * 1024),
        cost_estimate=pl.CostEstimate(flops=flops, transcendentals=0, bytes_accessed=1000000),
    )


def pack_kernel(slots, pos, vel, spin, rad, pool, send):
    for c in range(3):
        pool[c] = pos[c]
        pool[3 + c] = vel[c]
        pool[6 + c] = spin[c]
    pool[9] = rad[...]
    for j in range(MOVE):
        s = slots[0, j]
        for c in range(3):
            send[c, j : j + 1, :] = pos[c, pl.ds(s, 1), :]
            send[3 + c, j : j + 1, :] = vel[c, pl.ds(s, 1), :]
            send[6 + c, j : j + 1, :] = spin[c, pl.ds(s, 1), :]
        send[9, j : j + 1, :] = rad[pl.ds(s, 1), :]


def table_kernel(counts, slots, ghosts, corners, tab, lev, code, level):
    def init(i, _):
        for k in range(8):
            code[8 * i + k] = 8 * i + k
            level[8 * i + k] = 0
        return 0

    lax.fori_loop(0, S // 8, init, 0)

    def move(t, _):
        live = counts[t]

        def one(i, _):
            for k in range(4):
                j = 4 * i + k
                s = slots[t, j]
                old = code[s]
                tab[T_SEND + MOVE * t + j] = old
                code[s] = jnp.where(j < live, S + MOVE * t + j, old)
                level[s] = jnp.where(j < live, t + 1, level[s])
            return 0

        lax.fori_loop(0, MOVE // 4, one, 0)
        return 0

    lax.fori_loop(0, BITS, move, 0)

    def final(i, _):
        for k in range(8):
            e = 8 * i + k
            tab[T_FINAL + e] = code[e]
            lev[e] = level[e]
        return 0

    lax.fori_loop(0, S // 8, final, 0)
    for k in range(4):

        def face(i, _, k=k):
            for g in range(8):
                tab[T_GHOST + GHOST * k + 8 * i + g] = code[ghosts[k, 8 * i + g]]
            return 0

        lax.fori_loop(0, GHOST // 8, face, 0)
        for g in range(CORNER):
            tab[T_CORNER + CORNER * k + g] = code[corners[k, g]]


def order_kernel(tab, lev, first, second, live_ref, out, cat, start):
    live = live_ref[0, 0]
    even_w = odd("wid") == 0
    even_l = odd("len") == 0
    for k in range(CATS):
        start[k] = 0

    def sort_in(e, _):
        b = second[e]
        own = b < S
        ready = jnp.maximum(lev[first[e]], lev[jnp.minimum(b, S - 1)])
        g = b - S
        wide = (g >= GHOST) & (g < 3 * GHOST)
        where = jnp.where(own, ready, jnp.where(wide, 9, 10))
        cat[e] = where
        start[where] = start[where] + 1
        return 0

    lax.fori_loop(0, live, sort_in, 0)
    total = jnp.int32(0)
    done = jnp.int32(0)
    for k in range(CATS):
        n = start[k]
        start[k] = total
        total = total + n
        if k < BITS:
            if k >= FIRST_WINDOW:
                done = jnp.minimum(total, done + CAP)
            out[Q_END + k] = done
        else:
            out[Q_END + k] = total

    def place(e, _):
        where = cat[e]
        at = start[where]
        start[where] = at + 1
        a = first[e]
        b = second[e]
        out[Q_SLOT + at] = a
        out[Q_A + at] = tab[T_FINAL + a]
        g = b - S
        face = g // GHOST
        wide = jnp.where((face == 1) == even_w, G_WA, G_WB) + g - face * GHOST
        h = g - 4 * GHOST
        k = h // CORNER
        low = jnp.where(face < 4, face == 0, k < 2)
        along = jnp.where(low == even_l, G_LA, G_LB)
        along = along + jnp.where(face < 4, g - face * GHOST, GHOST + h - jnp.where(k < 2, 0, 2 * CORNER))
        ghost = jnp.where((face == 1) | (face == 2), wide, along)
        out[Q_B + at] = jnp.where(b < S, tab[T_FINAL + jnp.minimum(b, S - 1)], ghost + GBASE)
        return 0

    lax.fori_loop(0, live, place, 0)


def gather_rows(everything, tab, base, count, out, at):
    for j in range(count):
        s = tab[base + j]
        for c in range(ROWS):
            out[c, at + j : at + j + 1, :] = everything[c, pl.ds(s, 1), :]


def fill(everything, pool, received):
    everything[:, 0:OWN, :] = pool[...]
    for k, part in enumerate(received):
        everything[:, OWN + MOVE * k : OWN + MOVE * (k + 1), :] = part[...]


def step_kernel(t, tab, pool, *rest):
    received, send, everything = rest[:t], rest[-2], rest[-1]
    fill(everything, pool, received)
    gather_rows(everything, tab, T_SEND + MOVE * t, MOVE, send, 0)


def odd(axis):
    return lax.rem(lax.axis_index(axis), 2)


def ghost_wide_kernel(tab, pool, *rest):
    received = rest[:BITS]
    first, second, everything = rest[-3:]
    fill(everything, pool, received)
    up = 1 - odd("wid")
    for out, k in ((first, up), (second, 1 - up)):
        gather_rows(everything, tab, T_GHOST + GHOST * (1 + k), GHOST, out, 0)
        gather_rows(everything, tab, T_CORNER + CORNER * k, CORNER, out, GHOST)
        gather_rows(everything, tab, T_CORNER + CORNER * (2 + k), CORNER, out, GHOST + CORNER)


def ghost_long_kernel(tab, pool, *rest):
    received = rest[:BITS]
    wa, wb = rest[BITS : BITS + 2]
    first, second, everything = rest[-3:]
    fill(everything, pool, received)
    up = 1 - odd("len")
    flip = odd("wid")
    for out, k in ((first, up), (second, 1 - up)):
        gather_rows(everything, tab, T_GHOST + 3 * GHOST * k, GHOST, out, 0)
        for c in range(ROWS):
            at = pl.ds(GHOST + CORNER * k, CORNER)
            a, b = wa[c, at, :], wb[c, at, :]
            swap = jnp.full((CORNER, BLK), flip) == 1
            out[c, GHOST : GHOST + CORNER, :] = jnp.where(swap, b, a)
            out[c, GHOST + CORNER : WIDE, :] = jnp.where(swap, a, b)


def pair_rows(everything, a, b):
    near = [jnp.broadcast_to(everything[c, pl.ds(a, 1), :], (8, BLK)) for c in range(ROWS)]
    far = [jnp.broadcast_to(everything[c, pl.ds(b, 1), :], (8, BLK)) for c in range(ROWS)]
    px, py, pz, vx, vy, vz, wx, wy, wz, rad = near
    sx, sy, sz = wx * rad, wy * rad, wz * rad
    far[6:9] = [far[6] * far[9], far[7] * far[9], far[8] * far[9]]
    base = [pltpu.roll(x, 0, 1, stride=1, stride_axis=0) for x in far]
    acc = None
    for m in range(BLK // 8):
        qx, qy, qz, ux, uy, uz, tx, ty, tz, b_rad = [
            pltpu.roll(x, 8 * m, 1) if m else x for x in base
        ]
        rx, ry, rz = qx - px, qy - py, qz - pz
        d2 = (rx * rx + ry * ry) + (rz * rz + 0.01)
        inv = lax.rsqrt(d2)
        delta = jnp.maximum((rad + b_rad) - d2 * inv, 0.0)
        root = delta * lax.rsqrt(jnp.maximum(delta, 1e-30))
        nx, ny, nz = rx * inv, ry * inv, rz * inv
        ax, ay, az = sx + tx, sy + ty, sz + tz
        dx, dy, dz = ux - vx, uy - vy, uz - vz
        ex = (dx - ay * nz) + az * ny
        ey = (dy - az * nx) + ax * nz
        ez = (dz - ax * ny) + ay * nx
        un = (ex * nx + ey * ny) + ez * nz
        g = jnp.maximum(root * (30.0 * delta - un), 0.0)
        gx, gy, gz = ex - un * nx, ey - un * ny, ez - un * nz
        c = g * lax.rsqrt((gx * gx + gy * gy) + (gz * gz + 0.01))
        cx, cy, cz = c * gx, c * gy, c * gz
        terms = [cx, cy, cz, g * nx, g * ny, g * nz]
        terms += [ny * cz - nz * cy, nz * cx - nx * cz, nx * cy - ny * cx]
        acc = terms if acc is None else [p + q for p, q in zip(acc, terms)]
    acc = [jnp.sum(x, axis=0, keepdims=True) for x in acc]
    force = [10.0 * acc[k] - 20.0 * acc[3 + k] for k in range(3)]
    scale = 10.0 * rad[0:1, :]
    torque = [scale * acc[6 + k] for k in range(3)]
    return force + torque


def early_kernel(t, pairs, pool, *rest):
    received, rows, everything = rest[:t], rest[t], rest[t + 1]
    low = pairs[Q_END + t - 1]
    high = pairs[Q_END + t]

    @pl.when(high > low)
    def _():
        fill(everything, pool, received)

        def one(e, _):
            values = pair_rows(everything, pairs[Q_A + e], pairs[Q_B + e])
            for k in range(6):
                rows[k, pl.ds(e - low, 1), :] = values[k]
            return 0

        lax.fori_loop(low, high, one, 0)


def add_pair(everything, totals, pairs, e):
    values = pair_rows(everything, pairs[Q_A + e], pairs[Q_B + e])
    s = pairs[Q_SLOT + e]
    for k in range(6):
        totals[k, pl.ds(s, 1), :] = totals[k, pl.ds(s, 1), :] + values[k]


def middle_kernel(pairs, tab, pool, *rest):
    received = rest[:BITS]
    windows = BITS - FIRST_WINDOW
    early = rest[BITS : BITS + windows]
    state, totals, everything = rest[BITS + windows :]
    fill(everything, pool, received)

    def settle(i, _):
        for k in range(4):
            s = 4 * i + k
            at = tab[T_FINAL + s]
            for c in range(ROWS):
                state[c, pl.ds(s, 1), :] = everything[c, pl.ds(at, 1), :]
        return 0

    lax.fori_loop(0, S // 4, settle, 0)
    totals[...] = jnp.zeros((6, S, BLK), jnp.float32)
    for w, rows in enumerate(early):
        low = pairs[Q_END + FIRST_WINDOW + w - 1]
        high = pairs[Q_END + FIRST_WINDOW + w]

        def add(e, _, low=low, rows=rows):
            s = pairs[Q_SLOT + e]
            for k in range(6):
                totals[k, pl.ds(s, 1), :] = totals[k, pl.ds(s, 1), :] + rows[k, pl.ds(e - low, 1), :]
            return 0

        lax.fori_loop(low, high, add, 0)

    def one(e, _):
        add_pair(everything, totals, pairs, e)
        return 0

    lax.fori_loop(pairs[Q_END + BITS - 1], pairs[Q_END + BITS], one, 0)


def add_pairs(everything, totals, pairs, low, high, shift):
    def one(e, _):
        s = pairs[Q_SLOT + e]
        values = pair_rows(everything, s, pairs[Q_B + e] - shift)
        for k in range(6):
            totals[k, pl.ds(s, 1), :] = totals[k, pl.ds(s, 1), :] + values[k]
        return 0

    lax.fori_loop(low, high, one, 0)


def wide_kernel(pairs, state, wa, wb, totals_in, totals, everything):
    totals[...] = totals_in[...]
    everything[:, 0:OWN, :] = state[...]
    everything[:, OWN + G_WA : OWN + G_WA + GHOST, :] = wa[:, 0:GHOST, :]
    everything[:, OWN + G_WB : OWN + G_WB + GHOST, :] = wb[:, 0:GHOST, :]
    add_pairs(everything, totals, pairs, pairs[Q_END + 8], pairs[Q_END + 9], GBASE - OWN)


def last_kernel(pairs, state, la, lb, totals_in, pos, vel, spin, rad, totals, everything):
    totals[...] = totals_in[...]
    everything[:, 0:OWN, :] = state[...]
    everything[:, OWN : OWN + WIDE, :] = la[...]
    everything[:, OWN + WIDE : OWN + 2 * WIDE, :] = lb[...]
    add_pairs(everything, totals, pairs, pairs[Q_END + 9], pairs[Q_END + 10], GBASE + G_LA - OWN)
    a = state[9]
    mass = (DENSITY * (4.0 / 3.0) * math.pi) * a * a * a
    inertia = 0.4 * mass * a * a
    by_mass = TIME_STEP / mass
    by_inertia = TIME_STEP / inertia
    for c in range(3):
        v = state[3 + c] + totals[c] * by_mass
        vel[c] = v
        pos[c] = state[c] + TIME_STEP * v
        spin[c] = state[6 + c] + totals[3 + c] * by_inertia
    rad[...] = a


def neighbours(size, low):
    pairs = [(i, i + 1) for i in range(low, size - 1, 2)]
    return pairs + [(j, i) for i, j in pairs]


def kept(x):
    return pltpu.with_memory_space_constraint(x, pltpu.VMEM)


def body(
    positions,
    velocities,
    spins,
    sphere_radii,
    swap_counts,
    swap_slots,
    ghost_slots,
    corner_slots,
    pair_first,
    pair_second,
    pair_live,
):
    n_len = lax.axis_size("len")
    n_wid = lax.axis_size("wid")
    planes = [x[0, 0].transpose(1, 0, 2) for x in (positions, velocities, spins)]
    counts = swap_counts[0, 0]
    slots = swap_slots[0, 0]
    pool_t, send_t = vmem(ROWS, S, BLK), vmem(ROWS, MOVE, BLK)
    pool, send = call(
        pack_kernel, (pool_t, send_t), [SMEM] + [VMEM] * 4, (VMEM, VMEM), name="pack"
    )(slots, *planes, sphere_radii[0, 0])
    pool = kept(pool)
    ints = jax.ShapeDtypeStruct((T_SIZE,), jnp.int32)
    tab, lev = call(
        table_kernel,
        (ints, jax.ShapeDtypeStruct((S,), jnp.int32)),
        [SMEM] * 4,
        (SMEM, SMEM),
        [pltpu.SMEM((S,), jnp.int32)] * 2,
        name="tables",
        flops=2000000,
    )(counts, slots, ghost_slots[0, 0], corner_slots[0, 0])
    pairs = call(
        order_kernel,
        jax.ShapeDtypeStruct((Q_SIZE,), jnp.int32),
        [SMEM] * 5,
        SMEM,
        [pltpu.SMEM((PAIRS,), jnp.int32), pltpu.SMEM((16,), jnp.int32)],
        name="order",
        flops=2000000,
    )(tab, lev, pair_first[0, 0], pair_second[0, 0], pair_live)
    received, early = [], []
    for t in range(BITS):
        if t:
            behind = early[-1:] if t > FIRST_WINDOW else [pairs] if t == 2 else []
            send = call(
                functools.partial(step_kernel, t),
                send_t,
                [SMEM] + [VMEM] * (1 + t) + [ANY] * len(behind),
                VMEM,
                [pltpu.VMEM((ROWS, OWN + MOVE * t, BLK), jnp.float32)],
                name=f"step{t}",
            )(tab, pool, *received, *behind)
        axis, bit, size = ("len", t, n_len) if t < LBITS else ("wid", t - LBITS, n_wid)
        arrived = lax.ppermute(send, axis, [(i, i ^ (1 << bit)) for i in range(size)])
        if t >= FIRST_WINDOW:
            rows = (
                call(
                    functools.partial(early_kernel, t),
                    vmem(6, CAP_ROWS, BLK),
                    [SMEM] + [VMEM] * (1 + t),
                    VMEM,
                    [pltpu.VMEM((ROWS, OWN + MOVE * t, BLK), jnp.float32)],
                    name=f"early{t}",
                    flops=10000000,
                )(pairs, pool, *received)
            )
            early.append(kept(rows))
        received.append(kept(arrived))
    face_t = vmem(ROWS, WIDE, BLK)
    wa, wb = call(
        ghost_wide_kernel,
        (face_t, face_t),
        [SMEM] + [VMEM] * (1 + BITS) + [ANY],
        (VMEM, VMEM),
        [pltpu.VMEM((ROWS, OWN + RECV, BLK), jnp.float32)],
        name="ghosts_wid",
    )(tab, pool, *received, early[-1])
    wa = kept(lax.ppermute(wa, "wid", neighbours(n_wid, 0)))
    wb = kept(lax.ppermute(wb, "wid", neighbours(n_wid, 1)))
    totals_t = vmem(6, S, BLK)
    state, totals = call(
        middle_kernel,
        (pool_t, totals_t),
        [SMEM] * 2 + [VMEM] * (1 + BITS + BITS - FIRST_WINDOW),
        (VMEM, VMEM),
        [pltpu.VMEM((ROWS, OWN + RECV, BLK), jnp.float32)],
        name="middle",
        flops=10000000,
    )(pairs, tab, pool, *received, *early)
    state, totals = kept(state), kept(totals)
    la, lb = call(
        ghost_long_kernel,
        (face_t, face_t),
        [SMEM] + [VMEM] * (3 + BITS) + [ANY],
        (VMEM, VMEM),
        [pltpu.VMEM((ROWS, OWN + RECV, BLK), jnp.float32)],
        name="ghosts_len",
    )(tab, pool, *received, wa, wb, totals)
    la = kept(lax.ppermute(la, "len", neighbours(n_len, 0)))
    lb = kept(lax.ppermute(lb, "len", neighbours(n_len, 1)))
    totals = call(
        wide_kernel,
        totals_t,
        [SMEM] + [VMEM] * 4,
        VMEM,
        [pltpu.VMEM((ROWS, OWN + 2 * GHOST, BLK), jnp.float32)],
        name="wide",
        flops=10000000,
    )(pairs, state, wa, wb, totals)
    totals = kept(totals)
    out = call(
        last_kernel,
        (f32(3, S, BLK),) * 3 + (f32(S, BLK),),
        [SMEM] + [VMEM] * 4,
        (VMEM,) * 4,
        [pltpu.VMEM((6, S, BLK), jnp.float32), pltpu.VMEM((ROWS, OWN + 2 * WIDE, BLK), jnp.float32)],
        name="last",
    )(pairs, state, la, lb, totals)
    outs = [x.transpose(1, 0, 2)[None, None] for x in out[:3]]
    return (*outs, out[3][None, None])


def solution(mesh):
    five = P("len", "wid", None, None, None)
    four = P("len", "wid", None, None)
    three = P("len", "wid", None)
    in_specs = (five, five, five, four, three, four, four, four, three, three, P("len", "wid"))
    out_specs = (five, five, five, four)
    return jax.shard_map(body, mesh=mesh, in_specs=in_specs, out_specs=out_specs, check_vma=False)
```

```python
import functools
import math

import jax
import jax.numpy as jnp
from jax import lax
from jax.experimental import pallas as pl
from jax.experimental.pallas import tpu as pltpu
from jax.sharding import PartitionSpec as P

DENSITY = 1.9
TIME_STEP = 0.01
BLK = 128
S = 192
MOVE = 24
GHOST = 48
CORNER = 4
PAIRS = 128
BITS = 8
LBITS = 5
ROWS = 10
OWN = S
RECV = MOVE * BITS
WIDE = GHOST + 2 * CORNER
CORNERS = 2 * CORNER
G_WA, G_WB, G_LA, G_LB, G_CA, G_CB = 0, GHOST, 2 * GHOST, 3 * GHOST, 4 * GHOST, 4 * GHOST + CORNERS
GBASE = OWN + RECV
T_SEND, T_FINAL, T_GHOST, T_CORNER = 0, 192, 384, 576
T_SIZE = 640
Q_A, Q_B, Q_SLOT, Q_END = 0, 136, 272, 408
Q_SIZE = 512
CAPS = {2: 16, 3: 32, 4: 32, 6: 24, 7: 24}
CATS = 12
SPARE = 11
MARGIN = 0.02
UNROLL = 3

SMEM = pl.BlockSpec(memory_space=pltpu.SMEM)
VMEM = pl.BlockSpec(memory_space=pltpu.VMEM)
HBM = pl.BlockSpec(memory_space=pltpu.HBM)
ANY = pl.BlockSpec(memory_space=pl.ANY)


def f32(*shape):
    return jax.ShapeDtypeStruct(shape, jnp.float32)


def vmem(*shape):
    return pltpu.VMEM(shape, jnp.float32)


def call(body, out_shape, in_specs, out_specs, scratch=(), name=None, flops=0):
    return pl.pallas_call(
        body,
        out_shape=out_shape,
        in_specs=in_specs,
        out_specs=out_specs,
        scratch_shapes=list(scratch),
        name=name,
        compiler_params=pltpu.CompilerParams(vmem_limit_bytes=24 * 1024 * 1024),
        cost_estimate=pl.CostEstimate(flops=flops, transcendentals=0, bytes_accessed=1000000),
    )


def pack_kernel(slots_hbm, pos, vel, spin, rad, pool, send, slots, sems):
    copies = [
        pltpu.make_async_copy(slots_hbm, slots, sems.at[0]),
        pltpu.make_async_copy(pos, pool.at[0:3], sems.at[1]),
        pltpu.make_async_copy(vel, pool.at[3:6], sems.at[2]),
        pltpu.make_async_copy(spin, pool.at[6:9], sems.at[3]),
        pltpu.make_async_copy(rad, pool.at[9], sems.at[4]),
    ]
    for copy in copies:
        copy.start()
    for copy in copies:
        copy.wait()
    for j in range(MOVE):
        s = slots[0, j]
        for c in range(ROWS):
            send[c, j : j + 1, :] = pool[c, pl.ds(s, 1), :]


def table_kernel(counts, slots, ghosts, corners, tab, code):
    def init(i, _):
        for k in range(16):
            code[16 * i + k] = 16 * i + k
        return 0

    lax.fori_loop(0, S // 16, init, 0)

    def move(t, _):
        live = counts[t]

        def one(i, _):
            first = 8 * i
            places = [slots[t, first + k] for k in range(8)]
            olds = [code[s] for s in places]
            for k in range(8):
                tab[T_SEND + MOVE * t + first + k] = olds[k]
            for k in range(8):
                j = first + k
                code[places[k]] = jnp.where(j < live, S + MOVE * t + j, olds[k])
            return 0

        lax.fori_loop(0, MOVE // 8, one, 0)
        return 0

    lax.fori_loop(0, BITS, move, 0)

    def final(i, _):
        values = [code[8 * i + k] for k in range(8)]
        for k in range(8):
            tab[T_FINAL + 8 * i + k] = values[k]
        return 0

    lax.fori_loop(0, S // 8, final, 0)
    for k in range(4):

        def face(i, _, k=k):
            values = [code[ghosts[k, 8 * i + g]] for g in range(8)]
            for g in range(8):
                tab[T_GHOST + GHOST * k + 8 * i + g] = values[g]
            return 0

        lax.fori_loop(0, GHOST // 8, face, 0)
        for g in range(CORNER):
            tab[T_CORNER + CORNER * k + g] = code[corners[k, g]]


def order_kernel(tab, first, second, live_ref, out, cat, start):
    live = live_ref[0, 0]
    even_w = odd("wid") == 0
    even_l = odd("len") == 0
    for k in range(CATS):
        start[k] = 0
    groups = (live + 3) // 4

    def sort_in(i, _):
        cats = []
        for k in range(4):
            e = 4 * i + k
            b = second[e]
            code = jnp.maximum(tab[T_FINAL + first[e]], tab[T_FINAL + jnp.minimum(b, S - 1)])
            ready = jnp.where(code < S, 0, ((code - S) * 171 >> 12) + 1)
            g = b - S
            wide = (g >= GHOST) & (g < 3 * GHOST)
            where = jnp.where(b < S, ready, jnp.where(wide, 9, 10))
            cats.append(jnp.where(e < live, where, SPARE))
        for k in range(4):
            cat[4 * i + k] = cats[k]
        for k in range(4):
            start[cats[k]] = start[cats[k]] + 1
        return 0

    lax.fori_loop(0, groups, sort_in, 0)
    total = jnp.int32(0)
    done = jnp.int32(0)
    for k in range(CATS):
        n = start[k]
        start[k] = total
        total = total + n
        if k < BITS:
            done = jnp.minimum(total, done + CAPS.get(k, 0))
            out[Q_END + k] = done
        else:
            out[Q_END + k] = total

    def place(i, _):
        spots = []
        for k in range(4):
            e = 4 * i + k
            a = first[e]
            b = second[e]
            g = b - S
            h = g - 4 * GHOST
            diagonal = h >= 0
            face = jnp.where(g < GHOST, 0, jnp.where(g < 2 * GHOST, 1, jnp.where(g < 3 * GHOST, 2, 3)))
            low = jnp.where(diagonal, h < 2 * CORNER, face < 2)
            wide = (face == 1) | (face == 2)
            ahead = jnp.where(wide & (h < 0), low == even_w, low == even_l)
            start_at = jnp.where(wide, G_WA, G_LA) + jnp.where(ahead, 0, GHOST) + g - face * GHOST
            corner_at = G_CA + jnp.where(ahead, 0, CORNERS) + h - jnp.where(low, 0, CORNERS)
            ghost = jnp.where(diagonal, corner_at, start_at) + GBASE
            own = tab[T_FINAL + jnp.minimum(b, S - 1)]
            spots.append((cat[e], a, tab[T_FINAL + a], jnp.where(b < S, own, ghost)))
        for where, a, near, far in spots:
            at = start[where]
            start[where] = at + 1
            out[Q_SLOT + at] = a
            out[Q_A + at] = near
            out[Q_B + at] = far
        return 0

    lax.fori_loop(0, groups, place, 0)


def gather_rows(everything, tab, base, count, out, at):
    for j in range(count):
        s = tab[base + j]
        for c in range(ROWS):
            out[c, at + j : at + j + 1, :] = everything[c, pl.ds(s, 1), :]


def fill(everything, pool, received):
    everything[:, 0:OWN, :] = pool[...]
    for k, part in enumerate(received):
        everything[:, OWN + MOVE * k : OWN + MOVE * (k + 1), :] = part[...]


def step_kernel(t, tab, pool, *rest):
    received, send, everything = rest[:t], rest[-2], rest[-1]
    fill(everything, pool, received)
    gather_rows(everything, tab, T_SEND + MOVE * t, MOVE, send, 0)


def odd(axis):
    return lax.rem(lax.axis_index(axis), 2)


def ghost_kernel(tab, pool, *rest):
    received = rest[:BITS]
    la, lb, wa, wb, everything = rest[-5:]
    fill(everything, pool, received)
    up = 1 - odd("wid")
    for out, k in ((wa, up), (wb, 1 - up)):
        gather_rows(everything, tab, T_GHOST + GHOST * (1 + k), GHOST, out, 0)
        gather_rows(everything, tab, T_CORNER + CORNER * k, CORNER, out, GHOST)
        gather_rows(everything, tab, T_CORNER + CORNER * (2 + k), CORNER, out, GHOST + CORNER)
    up = 1 - odd("len")
    for out, k in ((la, up), (lb, 1 - up)):
        gather_rows(everything, tab, T_GHOST + 3 * GHOST * k, GHOST, out, 0)


def corner_kernel(wa, wb, _, ca, cb):
    up = 1 - odd("len")
    flip = odd("wid")
    swap = jnp.full((CORNER, BLK), flip) == 1
    for out, k in ((ca, up), (cb, 1 - up)):
        for c in range(ROWS):
            at = pl.ds(GHOST + CORNER * k, CORNER)
            a, b = wa[c, at, :], wb[c, at, :]
            out[c, 0:CORNER, :] = jnp.where(swap, b, a)
            out[c, CORNER:CORNERS, :] = jnp.where(swap, a, b)


def rounded(x):
    return x.astype(jnp.bfloat16).astype(jnp.float32)


def factor(x, y, z, a, sub, near):
    pick = (sub & 1) == 0 if near else (sub & 2) == 0
    out = []
    for v in (jnp.where(sub < 4, x, y), jnp.where(sub < 4, z, a)):
        high = rounded(v)
        w = jnp.where(pick, high, v - high)
        out.append(w + w if near else w)
    c = a * a - ((x * x + y * y) + z * z)
    if near:
        c = c + MARGIN
    c1 = rounded(c)
    rest = c - c1
    c2 = rounded(rest)
    c3 = rest - c2
    b = 3 if near else 0
    ones = sub < 3 if near else (sub >= 3) & (sub < 6)
    tail = jnp.where(sub == b + 2, c3, jnp.where(ones, 1.0, 0.0))
    out.append(jnp.where(sub == b, c1, jnp.where(sub == b + 1, c2, tail)))
    out.append(jnp.zeros_like(x))
    return jnp.concatenate(out, axis=0).astype(jnp.bfloat16)


def contact(near, far, touching):
    px, py, pz, vx, vy, vz, sx, sy, sz, a = near
    qx, qy, qz, ux, uy, uz, tx, ty, tz, b = far
    rx, ry, rz = qx - px, qy - py, qz - pz
    d2 = (rx * rx + ry * ry) + (rz * rz + 0.01)
    inv = lax.rsqrt(d2)
    delta = jnp.maximum((a + b) - d2 * inv, 0.0)
    root = delta * lax.rsqrt(jnp.maximum(delta, 1e-30))
    nx, ny, nz = rx * inv, ry * inv, rz * inv
    wx, wy, wz = sx + tx, sy + ty, sz + tz
    dx, dy, dz = ux - vx, uy - vy, uz - vz
    ex = (dx - wy * nz) + wz * ny
    ey = (dy - wz * nx) + wx * nz
    ez = (dz - wx * ny) + wy * nx
    un = (ex * nx + ey * ny) + ez * nz
    g = jnp.where(touching, jnp.maximum(root * (30.0 * delta - un), 0.0), 0.0)
    gx, gy, gz = ex - un * nx, ey - un * ny, ez - un * nz
    c = g * lax.rsqrt((gx * gx + gy * gy) + (gz * gz + 0.01))
    cx, cy, cz = c * gx, c * gy, c * gz
    force = [cx, cy, cz, g * nx, g * ny, g * nz]
    return force + [ny * cz - nz * cy, nz * cx - nx * cz, nx * cy - ny * cx]


def eight_pairs(everything, nears, fars, used, near_s, far_s, words):
    sub = lax.broadcasted_iota(jnp.int32, (8, BLK), 0)

    def row(c, i):
        return jnp.broadcast_to(everything[c, pl.ds(i, 1), :], (8, BLK))

    for u in range(8):
        a, b = nears[u], fars[u]
        for c in range(ROWS):
            near_s[c, u : u + 1, :] = everything[c, pl.ds(a, 1), :]
            far_s[c, u : u + 1, :] = everything[c, pl.ds(b, 1), :]
        left = factor(*[row(c, b) for c in (0, 1, 2, 9)], sub, False)
        right = factor(*[row(c, a) for c in (0, 1, 2, 9)], sub, True)
        reach = lax.dot_general(
            left, right, (((0,), (0,)), ((), ())), preferred_element_type=jnp.float32
        )
        word = None
        for m in range(BLK // 8):
            bit = jnp.where(reach[8 * m : 8 * m + 8] > 0.0, 1 << m, 0)
            word = bit if word is None else word | bit
        word = word | (pltpu.roll(word, 4, 0) << 16)
        words[8 * u : 8 * u + 8, :] = word & used[u]
    left_over = [words[pl.ds(q, 8, stride=8), :] for q in range(4)]
    most = jnp.max(sum(lax.population_count(w) for w in left_over))

    def turned(x):
        return x[:6] + [x[6] * x[9], x[7] * x[9], x[8] * x[9], x[9]]

    near = turned([near_s[c] for c in range(ROWS)])
    far = turned([far_s[c] for c in range(ROWS)])

    def some(_, carry):
        w, acc = list(carry[:4]), list(carry[4:])
        for _ in range(UNROLL):
            some_in = [x != 0 for x in w[:3]]
            word = jnp.where(some_in[0], w[0], jnp.where(some_in[1], w[1], jnp.where(some_in[2], w[2], w[3])))
            q = jnp.where(some_in[0], 0, jnp.where(some_in[1], 1, jnp.where(some_in[2], 2, 3)))
            low = word & (-word)
            bit = 31 - lax.clz(low)
            w = [jnp.where(q == i, x ^ low, x) for i, x in enumerate(w)]
            j = (((bit & 15) << 3) + q + ((bit >> 4) << 2)) & (BLK - 1)
            terms = contact(near, [jnp.take_along_axis(x, j, axis=1) for x in far], low != 0)
            acc = [x + y for x, y in zip(acc, terms)]
        return (*w, *acc)

    zero = jnp.zeros((8, BLK), jnp.float32)
    passes = (most + UNROLL - 1) // UNROLL
    acc = lax.fori_loop(0, passes, some, (*left_over, *([zero] * 9)))[4:]
    force = [10.0 * acc[k] - 20.0 * acc[3 + k] for k in range(3)]
    scale = 10.0 * near[9]
    return force + [scale * acc[6 + k] for k in range(3)]


def all_pairs(everything, pairs, near_base, low, high, shift, scratch, sink):
    def group(i, _):
        at = [low + 8 * i + u for u in range(8)]
        inside = [jnp.minimum(e, high - 1) for e in at]
        used = [jnp.where(e < high, -1, 0) for e in at]
        nears = [pairs[near_base + e] for e in inside]
        fars = [pairs[Q_B + e] - shift for e in inside]
        sink(i, inside, eight_pairs(everything, nears, fars, used, *scratch))
        return 0

    lax.fori_loop(0, (high - low + 7) // 8, group, 0)


def early_kernel(t, pairs, pool, *rest):
    received, rows, everything, scratch = rest[:t], rest[t], rest[t + 1], rest[t + 2 :]
    low = pairs[Q_END + t - 1]
    high = pairs[Q_END + t]

    @pl.when(high > low)
    def _():
        fill(everything, pool, received)

        def sink(i, _, values):
            for k in range(6):
                rows[k, pl.ds(pl.multiple_of(8 * i, 8), 8), :] = values[k]

        all_pairs(everything, pairs, Q_A, low, high, 0, scratch, sink)


def into(totals, pairs):
    def sink(_, inside, values):
        for u in range(8):
            s = pairs[Q_SLOT + inside[u]]
            for k in range(6):
                totals[k, pl.ds(s, 1), :] = totals[k, pl.ds(s, 1), :] + values[k][u : u + 1]

    return sink


def middle_kernel(pairs, tab, pool, *rest):
    received = rest[:BITS]
    early = rest[BITS : BITS + len(CAPS)]
    state, totals, everything, *scratch = rest[BITS + len(CAPS) :]
    fill(everything, pool, received)

    def settle(i, _):
        for k in range(8):
            s = 8 * i + k
            at = tab[T_FINAL + s]
            for c in range(ROWS):
                state[c, pl.ds(s, 1), :] = everything[c, pl.ds(at, 1), :]
        return 0

    lax.fori_loop(0, S // 8, settle, 0)
    totals[...] = jnp.zeros((6, S, BLK), jnp.float32)
    for t, rows in zip(CAPS, early):
        low = pairs[Q_END + t - 1]
        high = pairs[Q_END + t]

        def add(e, _, low=low, rows=rows):
            s = pairs[Q_SLOT + e]
            for k in range(6):
                totals[k, pl.ds(s, 1), :] = totals[k, pl.ds(s, 1), :] + rows[k, pl.ds(e - low, 1), :]
            return 0

        lax.fori_loop(low, high, add, 0)
    low, high = pairs[Q_END + BITS - 1], pairs[Q_END + BITS]
    all_pairs(everything, pairs, Q_A, low, high, 0, scratch, into(totals, pairs))


def wide_kernel(pairs, state, wa, wb, totals_in, totals, everything, *scratch):
    totals[...] = totals_in[...]
    everything[:, 0:OWN, :] = state[...]
    everything[:, OWN : OWN + GHOST, :] = wa[:, 0:GHOST, :]
    everything[:, OWN + GHOST : OWN + 2 * GHOST, :] = wb[:, 0:GHOST, :]
    low, high = pairs[Q_END + 8], pairs[Q_END + 9]
    all_pairs(everything, pairs, Q_SLOT, low, high, GBASE - OWN, scratch, into(totals, pairs))


def last_kernel(pairs, state, la, lb, ca, cb, totals_in, pos, vel, spin, rad, totals, everything, *scratch):
    totals[...] = totals_in[...]
    everything[:, 0:OWN, :] = state[...]
    base = OWN - G_LA
    for at, part, n in ((G_LA, la, GHOST), (G_LB, lb, GHOST), (G_CA, ca, CORNERS), (G_CB, cb, CORNERS)):
        everything[:, base + at : base + at + n, :] = part[...]
    low, high = pairs[Q_END + 9], pairs[Q_END + 10]
    all_pairs(everything, pairs, Q_SLOT, low, high, GBASE - base, scratch, into(totals, pairs))
    a = state[9]
    mass = (DENSITY * (4.0 / 3.0) * math.pi) * a * a * a
    inertia = 0.4 * mass * a * a
    by_mass = TIME_STEP / mass
    by_inertia = TIME_STEP / inertia
    for c in range(3):
        v = state[3 + c] + totals[c] * by_mass
        vel[c] = v
        pos[c] = state[c] + TIME_STEP * v
        spin[c] = state[6 + c] + totals[3 + c] * by_inertia
    rad[...] = a


def neighbours(size, low):
    pairs = [(i, i + 1) for i in range(low, size - 1, 2)]
    return pairs + [(j, i) for i, j in pairs]


def kept(x):
    return pltpu.with_memory_space_constraint(x, pltpu.VMEM)


def stays(x):
    return pltpu.with_memory_space_constraint(x, pltpu.HBM)


def everything_of(rows):
    work = [pltpu.VMEM((ROWS, 8, BLK), jnp.float32)] * 2 + [pltpu.VMEM((64, BLK), jnp.int32)]
    return [pltpu.VMEM((ROWS, rows, BLK), jnp.float32)] + work


def body(
    positions,
    velocities,
    spins,
    sphere_radii,
    swap_counts,
    swap_slots,
    ghost_slots,
    corner_slots,
    pair_first,
    pair_second,
    pair_live,
):
    n_len = lax.axis_size("len")
    n_wid = lax.axis_size("wid")
    planes = [stays(x[0, 0].transpose(1, 0, 2)) for x in (positions, velocities, spins)]
    slots = swap_slots[0, 0]
    pool_t, send_t = vmem(ROWS, S, BLK), vmem(ROWS, MOVE, BLK)
    pool, send = call(
        pack_kernel,
        (pool_t, send_t),
        [HBM] * 5,
        (VMEM, VMEM),
        [pltpu.SMEM((BITS, MOVE), jnp.int32), pltpu.SemaphoreType.DMA((5,))],
        name="pack",
    )(stays(slots), *planes, stays(sphere_radii[0, 0]))
    pool = kept(pool)
    tab = call(
        table_kernel,
        jax.ShapeDtypeStruct((T_SIZE,), jnp.int32),
        [SMEM] * 4,
        SMEM,
        [pltpu.SMEM((S,), jnp.int32)],
        name="tables",
        flops=2000000,
    )(swap_counts[0, 0], slots, ghost_slots[0, 0], corner_slots[0, 0])
    pairs = call(
        order_kernel,
        jax.ShapeDtypeStruct((Q_SIZE,), jnp.int32),
        [SMEM] * 4,
        SMEM,
        [pltpu.SMEM((PAIRS,), jnp.int32), pltpu.SMEM((16,), jnp.int32)],
        name="order",
        flops=2000000,
    )(tab, pair_first[0, 0], pair_second[0, 0], pair_live)
    received, early = [], []
    behind = []
    for t in range(BITS):
        if t:
            send = call(
                functools.partial(step_kernel, t),
                send_t,
                [SMEM] + [VMEM] * (1 + t) + [ANY] * len(behind),
                VMEM,
                [pltpu.VMEM((ROWS, OWN + MOVE * t, BLK), jnp.float32)],
                name=f"step{t}",
            )(tab, pool, *received, *behind)
        axis, bit, size = ("len", t, n_len) if t < LBITS else ("wid", t - LBITS, n_wid)
        arrived = lax.ppermute(send, axis, [(i, i ^ (1 << bit)) for i in range(size)])
        behind = [pairs] if t == 1 else []
        if t in CAPS:
            rows = call(
                functools.partial(early_kernel, t),
                vmem(6, CAPS[t], BLK),
                [SMEM] + [VMEM] * (1 + t),
                VMEM,
                everything_of(OWN + MOVE * t),
                name=f"early{t}",
                flops=10000000,
            )(pairs, pool, *received)
            early.append(kept(rows))
            behind = early[-1:]
        received.append(kept(arrived))
    face_t, wide_t, corner_t = vmem(ROWS, GHOST, BLK), vmem(ROWS, WIDE, BLK), vmem(ROWS, CORNERS, BLK)
    la, lb, wa, wb = call(
        ghost_kernel,
        (face_t, face_t, wide_t, wide_t),
        [SMEM] + [VMEM] * (1 + BITS) + [ANY],
        (VMEM,) * 4,
        [pltpu.VMEM((ROWS, OWN + RECV, BLK), jnp.float32)],
        name="ghosts",
    )(tab, pool, *received, *behind)
    la = kept(lax.ppermute(la, "len", neighbours(n_len, 0)))
    lb = kept(lax.ppermute(lb, "len", neighbours(n_len, 1)))
    wa = kept(lax.ppermute(wa, "wid", neighbours(n_wid, 0)))
    wb = kept(lax.ppermute(wb, "wid", neighbours(n_wid, 1)))
    totals_t = vmem(6, S, BLK)
    state, totals = call(
        middle_kernel,
        (pool_t, totals_t),
        [SMEM] * 2 + [VMEM] * (1 + BITS + len(CAPS)),
        (VMEM, VMEM),
        everything_of(OWN + RECV),
        name="middle",
        flops=10000000,
    )(pairs, tab, pool, *received, *early)
    state, totals = kept(state), kept(totals)
    ca, cb = call(
        corner_kernel,
        (corner_t, corner_t),
        [VMEM] * 2 + [ANY],
        (VMEM, VMEM),
        name="corners",
    )(wa, wb, totals)
    ca = kept(lax.ppermute(ca, "len", neighbours(n_len, 0)))
    cb = kept(lax.ppermute(cb, "len", neighbours(n_len, 1)))
    totals = call(
        wide_kernel,
        totals_t,
        [SMEM] + [VMEM] * 4,
        VMEM,
        everything_of(OWN + 2 * GHOST),
        name="wide",
        flops=10000000,
    )(pairs, state, wa, wb, totals)
    out = call(
        last_kernel,
        (f32(3, S, BLK),) * 3 + (f32(S, BLK),),
        [SMEM] + [VMEM] * 6,
        (VMEM,) * 4,
        [pltpu.VMEM((6, S, BLK), jnp.float32)] + everything_of(OWN + 2 * GHOST + 2 * CORNERS),
        name="last",
    )(pairs, state, la, lb, ca, cb, kept(totals))
    outs = [x.transpose(1, 0, 2)[None, None] for x in out[:3]]
    return (*outs, out[3][None, None])


def solution(mesh):
    five = P("len", "wid", None, None, None)
    four = P("len", "wid", None, None)
    three = P("len", "wid", None)
    in_specs = (five, five, five, four, three, four, four, four, three, three, P("len", "wid"))
    out_specs = (five, five, five, four)
    return jax.shard_map(body, mesh=mesh, in_specs=in_specs, out_specs=out_specs, check_vma=False)
```

```python
import functools
import math

import jax
import jax.numpy as jnp
from jax import lax
from jax.experimental import pallas as pl
from jax.experimental.pallas import tpu as pltpu
from jax.sharding import PartitionSpec as P

DENSITY = 1.9
TIME_STEP = 0.01
BLK = 128
S = 192
MOVE = 24
GHOST = 48
CORNER = 4
PAIRS = 128
BITS = 8
LBITS = 5
ROWS = 10
OWN = S
RECV = MOVE * BITS
WIDE = GHOST + 2 * CORNER
CORNERS = 2 * CORNER
G_WA, G_WB, G_LA, G_LB = 0, GHOST, 2 * GHOST, 2 * GHOST + WIDE
GBASE = OWN + RECV
T_SEND, T_FINAL, T_SIZE = 0, 192, 512
G_FACE, G_CORNER, G_SIZE = 0, 192, 256
C_CAT, C_START, C_END, C_SIZE = 0, 128, 144, 256
Q_A, Q_B, Q_SLOT, Q_END = 0, 136, 272, 408
Q_SIZE = 512
CAPS = {3: 32, 4: 40, 6: 24, 7: 24}
CATS = 12
SPARE = 11
MARGIN = 0.02
UNROLL = 3

SMEM = pl.BlockSpec(memory_space=pltpu.SMEM)
VMEM = pl.BlockSpec(memory_space=pltpu.VMEM)
HBM = pl.BlockSpec(memory_space=pltpu.HBM)
ANY = pl.BlockSpec(memory_space=pl.ANY)


def f32(*shape):
    return jax.ShapeDtypeStruct(shape, jnp.float32)


def ints(size):
    return jax.ShapeDtypeStruct((size,), jnp.int32)


def vmem(*shape):
    return pltpu.VMEM(shape, jnp.float32)


def call(body, out_shape, in_specs, out_specs, scratch=(), name=None, flops=0, aliases=None):
    return pl.pallas_call(
        body,
        out_shape=out_shape,
        in_specs=in_specs,
        out_specs=out_specs,
        scratch_shapes=list(scratch),
        name=name,
        input_output_aliases=aliases or {},
        compiler_params=pltpu.CompilerParams(vmem_limit_bytes=24 * 1024 * 1024),
        cost_estimate=pl.CostEstimate(flops=flops, transcendentals=0, bytes_accessed=1000000),
    )


def pack_kernel(slots_hbm, pos, vel, spin, rad, pool, send, slots, sems):
    copies = [
        pltpu.make_async_copy(slots_hbm, slots, sems.at[0]),
        pltpu.make_async_copy(pos, pool.at[0:3], sems.at[1]),
        pltpu.make_async_copy(vel, pool.at[3:6], sems.at[2]),
        pltpu.make_async_copy(spin, pool.at[6:9], sems.at[3]),
        pltpu.make_async_copy(rad, pool.at[9], sems.at[4]),
    ]
    for copy in copies:
        copy.start()
    for copy in copies:
        copy.wait()
    for j in range(MOVE):
        s = slots[0, j]
        for c in range(ROWS):
            send[c, j : j + 1, :] = pool[c, pl.ds(s, 1), :]


def table_kernel(counts, slots, tab):
    def init(i, _):
        for k in range(16):
            tab[T_FINAL + 16 * i + k] = 16 * i + k
        return 0

    lax.fori_loop(0, S // 16, init, 0)

    def move(t, _):
        live = counts[t]

        def one(i, _):
            first = 8 * i
            places = [slots[t, first + k] for k in range(8)]
            olds = [tab[T_FINAL + s] for s in places]
            for k in range(8):
                tab[T_SEND + MOVE * t + first + k] = olds[k]
            for k in range(8):
                j = first + k
                tab[T_FINAL + places[k]] = jnp.where(j < live, S + MOVE * t + j, olds[k])
            return 0

        lax.fori_loop(0, MOVE // 8, one, 0)
        return 0

    lax.fori_loop(0, BITS, move, 0)


def ghost_table_kernel(tab, ghosts, corners, out):
    for k in range(4):

        def face(i, _, k=k):
            values = [tab[T_FINAL + ghosts[k, 8 * i + g]] for g in range(8)]
            for g in range(8):
                out[G_FACE + GHOST * k + 8 * i + g] = values[g]
            return 0

        lax.fori_loop(0, GHOST // 8, face, 0)
        for g in range(CORNER):
            out[G_CORNER + CORNER * k + g] = tab[T_FINAL + corners[k, g]]


def count_kernel(tab, first, second, live_ref, out, start):
    live = live_ref[0, 0]
    for k in range(CATS):
        start[k] = 0

    def sort_in(i, _):
        cats = []
        for k in range(4):
            e = 4 * i + k
            b = second[e]
            code = jnp.maximum(tab[T_FINAL + first[e]], tab[T_FINAL + jnp.minimum(b, S - 1)])
            ready = jnp.where(code < S, 0, ((code - S) * 171 >> 12) + 1)
            g = b - S
            wide = (g >= GHOST) & (g < 3 * GHOST)
            where = jnp.where(b < S, ready, jnp.where(wide, 9, 10))
            cats.append(jnp.where(e < live, where, SPARE))
        for k in range(4):
            out[C_CAT + 4 * i + k] = cats[k]
        for k in range(4):
            start[cats[k]] = start[cats[k]] + 1
        return 0

    lax.fori_loop(0, (live + 3) // 4, sort_in, 0)
    total = jnp.int32(0)
    done = jnp.int32(0)
    for k in range(CATS):
        out[C_START + k] = total
        total = total + start[k]
        if k < BITS:
            done = jnp.minimum(total, done + CAPS.get(k, 0))
            out[C_END + k] = done
        else:
            out[C_END + k] = total


def place_kernel(tab, cats, first, second, live_ref, out, start):
    live = live_ref[0, 0]
    even_w = odd("wid") == 0
    even_l = late() == 0
    for k in range(CATS):
        start[k] = cats[C_START + k]
        out[Q_END + k] = cats[C_END + k]

    def place(i, _):
        spots = []
        for k in range(4):
            e = 4 * i + k
            a = first[e]
            b = second[e]
            g = b - S
            h = g - 4 * GHOST
            diagonal = h >= 0
            face = jnp.where(g < GHOST, 0, jnp.where(g < 2 * GHOST, 1, jnp.where(g < 3 * GHOST, 2, 3)))
            low = jnp.where(diagonal, h < 2 * CORNER, face < 2)
            wide = (face == 1) | (face == 2)
            ahead = jnp.where(wide & (h < 0), low == even_w, low == even_l)
            wide_at = jnp.where(ahead, G_WA, G_WB) + g - face * GHOST
            inside = jnp.where(diagonal, GHOST + h - jnp.where(low, 0, CORNERS), g - face * GHOST)
            long_at = jnp.where(ahead, G_LA, G_LB) + inside
            ghost = jnp.where(wide & (h < 0), wide_at, long_at) + GBASE
            own = tab[T_FINAL + jnp.minimum(b, S - 1)]
            spots.append((cats[C_CAT + e], a, tab[T_FINAL + a], jnp.where(b < S, own, ghost)))
        for where, a, near, far in spots:
            at = start[where]
            start[where] = at + 1
            out[Q_SLOT + at] = a
            out[Q_A + at] = near
            out[Q_B + at] = far
        return 0

    lax.fori_loop(0, (live + 3) // 4, place, 0)


def gather_rows(everything, tab, base, count, out, at):
    for j in range(count):
        s = tab[base + j]
        for c in range(ROWS):
            out[c, at + j : at + j + 1, :] = everything[c, pl.ds(s, 1), :]


def fill(everything, pool, received):
    everything[:, 0:OWN, :] = pool[...]
    for k, part in enumerate(received):
        everything[:, OWN + MOVE * k : OWN + MOVE * (k + 1), :] = part[...]


def step_kernel(t, tab, pool, *rest):
    received, send, everything = rest[:t], rest[-2], rest[-1]
    fill(everything, pool, received)
    gather_rows(everything, tab, T_SEND + MOVE * t, MOVE, send, 0)


def odd(axis):
    return lax.rem(lax.axis_index(axis), 2)


def late():
    return lax.rem(lax.axis_index("len") + lax.axis_index("wid"), 2)


def wide_faces_kernel(tab, pool, *rest):
    wa, wb, everything = rest[-3:]
    fill(everything, pool, rest[:BITS])
    up = 1 - odd("wid")
    for out, k in ((wa, up), (wb, 1 - up)):
        gather_rows(everything, tab, G_FACE + GHOST * (1 + k), GHOST, out, 0)
        gather_rows(everything, tab, G_CORNER + CORNER * k, CORNER, out, GHOST)
        gather_rows(everything, tab, G_CORNER + CORNER * (2 + k), CORNER, out, GHOST + CORNER)


def long_faces_kernel(tab, pool, *rest):
    la, lb, everything = rest[-3:]
    fill(everything, pool, rest[:BITS])
    up = 1 - late()
    for out, k in ((la, up), (lb, 1 - up)):
        gather_rows(everything, tab, G_FACE + 3 * GHOST * k, GHOST, out, 0)


def forward_kernel(wa, wb, _, la_in, lb_in, la, lb):
    up = 1 - late()
    flip = odd("wid")
    swap = jnp.full((CORNER, BLK), flip) == 1
    for out, k in ((la, up), (lb, 1 - up)):
        for c in range(ROWS):
            at = pl.ds(GHOST + CORNER * k, CORNER)
            a, b = wa[c, at, :], wb[c, at, :]
            out[c, GHOST : GHOST + CORNER, :] = jnp.where(swap, b, a)
            out[c, GHOST + CORNER : WIDE, :] = jnp.where(swap, a, b)


def rounded(x):
    return x.astype(jnp.bfloat16).astype(jnp.float32)


def factor(x, y, z, a, sub, near):
    pick = (sub & 1) == 0 if near else (sub & 2) == 0
    out = []
    for v in (jnp.where(sub < 4, x, y), jnp.where(sub < 4, z, a)):
        high = rounded(v)
        w = jnp.where(pick, high, v - high)
        out.append(w + w if near else w)
    c = a * a - ((x * x + y * y) + z * z)
    if near:
        c = c + MARGIN
    c1 = rounded(c)
    rest = c - c1
    c2 = rounded(rest)
    c3 = rest - c2
    b = 3 if near else 0
    ones = sub < 3 if near else (sub >= 3) & (sub < 6)
    tail = jnp.where(sub == b + 2, c3, jnp.where(ones, 1.0, 0.0))
    out.append(jnp.where(sub == b, c1, jnp.where(sub == b + 1, c2, tail)))
    out.append(jnp.zeros_like(x))
    return jnp.concatenate(out, axis=0).astype(jnp.bfloat16)


def contact(near, far, touching):
    px, py, pz, vx, vy, vz, sx, sy, sz, a = near
    qx, qy, qz, ux, uy, uz, tx, ty, tz, b = far
    rx, ry, rz = qx - px, qy - py, qz - pz
    d2 = (rx * rx + ry * ry) + (rz * rz + 0.01)
    inv = lax.rsqrt(d2)
    delta = jnp.maximum((a + b) - d2 * inv, 0.0)
    root = delta * lax.rsqrt(jnp.maximum(delta, 1e-30))
    nx, ny, nz = rx * inv, ry * inv, rz * inv
    wx, wy, wz = sx + tx, sy + ty, sz + tz
    dx, dy, dz = ux - vx, uy - vy, uz - vz
    ex = (dx - wy * nz) + wz * ny
    ey = (dy - wz * nx) + wx * nz
    ez = (dz - wx * ny) + wy * nx
    un = (ex * nx + ey * ny) + ez * nz
    g = jnp.where(touching, jnp.maximum(root * (30.0 * delta - un), 0.0), 0.0)
    gx, gy, gz = ex - un * nx, ey - un * ny, ez - un * nz
    c = g * lax.rsqrt((gx * gx + gy * gy) + (gz * gz + 0.01))
    cx, cy, cz = c * gx, c * gy, c * gz
    force = [cx, cy, cz, g * nx, g * ny, g * nz]
    return force + [ny * cz - nz * cy, nz * cx - nx * cz, nx * cy - ny * cx]


def eight_pairs(everything, nears, fars, used, near_s, far_s, words):
    sub = lax.broadcasted_iota(jnp.int32, (8, BLK), 0)

    def row(c, i):
        return jnp.broadcast_to(everything[c, pl.ds(i, 1), :], (8, BLK))

    for u in range(8):
        a, b = nears[u], fars[u]
        for c in range(ROWS):
            near_s[c, u : u + 1, :] = everything[c, pl.ds(a, 1), :]
            far_s[c, u : u + 1, :] = everything[c, pl.ds(b, 1), :]
        left = factor(*[row(c, b) for c in (0, 1, 2, 9)], sub, False)
        right = factor(*[row(c, a) for c in (0, 1, 2, 9)], sub, True)
        reach = lax.dot_general(
            left, right, (((0,), (0,)), ((), ())), preferred_element_type=jnp.float32
        )
        word = None
        for m in range(BLK // 8):
            bit = jnp.where(reach[8 * m : 8 * m + 8] > 0.0, 1 << m, 0)
            word = bit if word is None else word | bit
        word = word | (pltpu.roll(word, 4, 0) << 16)
        words[8 * u : 8 * u + 8, :] = word & used[u]
    left_over = [words[pl.ds(q, 8, stride=8), :] for q in range(4)]
    most = jnp.max(sum(lax.population_count(w) for w in left_over))

    def turned(x):
        return x[:6] + [x[6] * x[9], x[7] * x[9], x[8] * x[9], x[9]]

    near = turned([near_s[c] for c in range(ROWS)])
    far = turned([far_s[c] for c in range(ROWS)])

    def some(_, carry):
        w, acc = list(carry[:4]), list(carry[4:])
        for _ in range(UNROLL):
            some_in = [x != 0 for x in w[:3]]
            word = jnp.where(some_in[0], w[0], jnp.where(some_in[1], w[1], jnp.where(some_in[2], w[2], w[3])))
            q = jnp.where(some_in[0], 0, jnp.where(some_in[1], 1, jnp.where(some_in[2], 2, 3)))
            low = word & (-word)
            bit = 31 - lax.clz(low)
            w = [jnp.where(q == i, x ^ low, x) for i, x in enumerate(w)]
            j = (((bit & 15) << 3) + q + ((bit >> 4) << 2)) & (BLK - 1)
            terms = contact(near, [jnp.take_along_axis(x, j, axis=1) for x in far], low != 0)
            acc = [x + y for x, y in zip(acc, terms)]
        return (*w, *acc)

    zero = jnp.zeros((8, BLK), jnp.float32)
    passes = (most + UNROLL - 1) // UNROLL
    acc = lax.fori_loop(0, passes, some, (*left_over, *([zero] * 9)))[4:]
    force = [10.0 * acc[k] - 20.0 * acc[3 + k] for k in range(3)]
    scale = 10.0 * near[9]
    return force + [scale * acc[6 + k] for k in range(3)]


def all_pairs(everything, pairs, near_base, low, high, shift, scratch, sink):
    def group(i, _):
        at = [low + 8 * i + u for u in range(8)]
        inside = [jnp.minimum(e, high - 1) for e in at]
        used = [jnp.where(e < high, -1, 0) for e in at]
        nears = [pairs[near_base + e] for e in inside]
        fars = [pairs[Q_B + e] - shift for e in inside]
        sink(i, inside, eight_pairs(everything, nears, fars, used, *scratch))
        return 0

    lax.fori_loop(0, (high - low + 7) // 8, group, 0)


def early_kernel(t, pairs, pool, *rest):
    received, rows, everything, scratch = rest[:t], rest[t], rest[t + 1], rest[t + 2 :]
    low = pairs[Q_END + t - 1]
    high = pairs[Q_END + t]

    @pl.when(high > low)
    def _():
        fill(everything, pool, received)

        def sink(i, _, values):
            for k in range(6):
                rows[k, pl.ds(pl.multiple_of(8 * i, 8), 8), :] = values[k]

        all_pairs(everything, pairs, Q_A, low, high, 0, scratch, sink)


def into(totals, pairs):
    def sink(_, inside, values):
        for u in range(8):
            s = pairs[Q_SLOT + inside[u]]
            for k in range(6):
                totals[k, pl.ds(s, 1), :] = totals[k, pl.ds(s, 1), :] + values[k][u : u + 1]

    return sink


def middle_kernel(pairs, tab, pool, *rest):
    received = rest[:BITS]
    early = rest[BITS : BITS + len(CAPS)]
    state, totals, everything, *scratch = rest[BITS + len(CAPS) :]
    fill(everything, pool, received)

    def settle(i, _):
        for k in range(8):
            s = 8 * i + k
            at = tab[T_FINAL + s]
            for c in range(ROWS):
                state[c, pl.ds(s, 1), :] = everything[c, pl.ds(at, 1), :]
        return 0

    lax.fori_loop(0, S // 8, settle, 0)
    totals[...] = jnp.zeros((6, S, BLK), jnp.float32)
    for t, rows in zip(CAPS, early):
        low = pairs[Q_END + t - 1]
        high = pairs[Q_END + t]

        def add(e, _, low=low, rows=rows):
            s = pairs[Q_SLOT + e]
            for k in range(6):
                totals[k, pl.ds(s, 1), :] = totals[k, pl.ds(s, 1), :] + rows[k, pl.ds(e - low, 1), :]
            return 0

        lax.fori_loop(low, high, add, 0)
    low, high = pairs[Q_END + BITS - 1], pairs[Q_END + BITS]
    all_pairs(everything, pairs, Q_A, low, high, 0, scratch, into(totals, pairs))


def wide_kernel(pairs, state, wa, wb, totals_in, totals, everything, *scratch):
    totals[...] = totals_in[...]
    everything[:, 0:OWN, :] = state[...]
    everything[:, OWN : OWN + GHOST, :] = wa[:, 0:GHOST, :]
    everything[:, OWN + GHOST : OWN + 2 * GHOST, :] = wb[:, 0:GHOST, :]
    low, high = pairs[Q_END + 8], pairs[Q_END + 9]
    all_pairs(everything, pairs, Q_SLOT, low, high, GBASE - OWN, scratch, into(totals, pairs))


def last_kernel(pairs, state, la, lb, totals_in, pos, vel, spin, rad, totals, everything, *scratch):
    totals[...] = totals_in[...]
    everything[:, 0:OWN, :] = state[...]
    everything[:, OWN : OWN + WIDE, :] = la[...]
    everything[:, OWN + WIDE : OWN + 2 * WIDE, :] = lb[...]
    low, high = pairs[Q_END + 9], pairs[Q_END + 10]
    shift = GBASE + G_LA - OWN
    all_pairs(everything, pairs, Q_SLOT, low, high, shift, scratch, into(totals, pairs))
    a = state[9]
    mass = (DENSITY * (4.0 / 3.0) * math.pi) * a * a * a
    inertia = 0.4 * mass * a * a
    by_mass = TIME_STEP / mass
    by_inertia = TIME_STEP / inertia
    for c in range(3):
        v = state[3 + c] + totals[c] * by_mass
        vel[c] = v
        pos[c] = state[c] + TIME_STEP * v
        spin[c] = state[6 + c] + totals[3 + c] * by_inertia
    rad[...] = a


def neighbours(size, low):
    pairs = [(i, i + 1) for i in range(low, size - 1, 2)]
    return pairs + [(j, i) for i, j in pairs]


def long_neighbours(n_len, n_wid, second):
    route = []
    for i in range(n_len):
        for w in range(n_wid):
            j = i + 1 if (i + w + second) % 2 == 0 else i - 1
            if 0 <= j < n_len:
                route.append((i * n_wid + w, j * n_wid + w))
    return route


def kept(x):
    return pltpu.with_memory_space_constraint(x, pltpu.VMEM)


def stays(x):
    return pltpu.with_memory_space_constraint(x, pltpu.HBM)


def everything_of(rows):
    work = [pltpu.VMEM((ROWS, 8, BLK), jnp.float32)] * 2 + [pltpu.VMEM((64, BLK), jnp.int32)]
    return [pltpu.VMEM((ROWS, rows, BLK), jnp.float32)] + work


def body(
    positions,
    velocities,
    spins,
    sphere_radii,
    swap_counts,
    swap_slots,
    ghost_slots,
    corner_slots,
    pair_first,
    pair_second,
    pair_live,
):
    n_len = lax.axis_size("len")
    n_wid = lax.axis_size("wid")
    planes = [stays(x[0, 0].transpose(1, 0, 2)) for x in (positions, velocities, spins)]
    slots = swap_slots[0, 0]
    pool_t, send_t = vmem(ROWS, S, BLK), vmem(ROWS, MOVE, BLK)
    pool, send = call(
        pack_kernel,
        (pool_t, send_t),
        [HBM] * 5,
        (VMEM, VMEM),
        [pltpu.SMEM((BITS, MOVE), jnp.int32), pltpu.SemaphoreType.DMA((5,))],
        name="pack",
    )(stays(slots), *planes, stays(sphere_radii[0, 0]))
    pool = kept(pool)
    lists = (pair_first[0, 0], pair_second[0, 0], pair_live)
    counter = [pltpu.SMEM((16,), jnp.int32)]
    tab = call(table_kernel, ints(T_SIZE), [SMEM] * 2, SMEM, name="tables", flops=2000000)(
        swap_counts[0, 0], slots
    )
    cats = call(count_kernel, ints(C_SIZE), [SMEM] * 4, SMEM, counter, "count", 2000000)(tab, *lists)
    pairs = call(place_kernel, ints(Q_SIZE), [SMEM] * 5, SMEM, counter, "place", 2000000)(
        tab, cats, *lists
    )
    gtab = call(ghost_table_kernel, ints(G_SIZE), [SMEM] * 3, SMEM, name="ghost_table", flops=1000000)(
        tab, ghost_slots[0, 0], corner_slots[0, 0]
    )
    windows = {1: [cats], 2: [pairs], 4: [gtab]}
    received, early = [], []
    behind = []
    for t in range(BITS):
        if t:
            send = call(
                functools.partial(step_kernel, t),
                send_t,
                [SMEM] + [VMEM] * (1 + t) + [ANY] * len(behind),
                VMEM,
                [pltpu.VMEM((ROWS, OWN + MOVE * t, BLK), jnp.float32)],
                name=f"step{t}",
            )(tab, pool, *received, *behind)
        axis, bit, size = ("len", t, n_len) if t < LBITS else ("wid", t - LBITS, n_wid)
        arrived = lax.ppermute(send, axis, [(i, i ^ (1 << bit)) for i in range(size)])
        behind = list(windows.get(t, []))
        if t in CAPS:
            rows = call(
                functools.partial(early_kernel, t),
                vmem(6, CAPS[t], BLK),
                [SMEM] + [VMEM] * (1 + t),
                VMEM,
                everything_of(OWN + MOVE * t),
                name=f"early{t}",
                flops=10000000,
            )(pairs, pool, *received)
            early.append(kept(rows))
            behind.append(early[-1])
        received.append(kept(arrived))
    wide_t = vmem(ROWS, WIDE, BLK)
    faces = [pltpu.VMEM((ROWS, OWN + RECV, BLK), jnp.float32)]
    wa, wb = call(
        wide_faces_kernel,
        (wide_t, wide_t),
        [SMEM] + [VMEM] * (1 + BITS) + [ANY] * len(behind),
        (VMEM, VMEM),
        faces,
        name="wide_faces",
    )(gtab, pool, *received, *behind)
    sent = kept(wa)
    wa = kept(lax.ppermute(wa, "wid", neighbours(n_wid, 0)))
    wb = kept(lax.ppermute(wb, "wid", neighbours(n_wid, 1)))
    la, lb = call(
        long_faces_kernel,
        (wide_t, wide_t),
        [SMEM] + [VMEM] * (1 + BITS) + [ANY],
        (VMEM, VMEM),
        faces,
        name="long_faces",
        flops=1000000,
    )(gtab, pool, *received, sent)
    totals_t = vmem(6, S, BLK)
    state, totals = call(
        middle_kernel,
        (pool_t, totals_t),
        [SMEM] * 2 + [VMEM] * (1 + BITS + len(CAPS)),
        (VMEM, VMEM),
        everything_of(OWN + RECV),
        name="middle",
        flops=10000000,
    )(pairs, tab, pool, *received, *early)
    state, totals = kept(state), kept(totals)
    la, lb = call(
        forward_kernel,
        (wide_t, wide_t),
        [VMEM] * 2 + [ANY] + [VMEM] * 2,
        (VMEM, VMEM),
        name="forward",
        aliases={3: 0, 4: 1},
    )(wa, wb, totals, kept(la), kept(lb))
    la = kept(lax.ppermute(la, ("len", "wid"), long_neighbours(n_len, n_wid, 0)))
    lb = kept(lax.ppermute(lb, ("len", "wid"), long_neighbours(n_len, n_wid, 1)))
    totals = call(
        wide_kernel,
        totals_t,
        [SMEM] + [VMEM] * 4,
        VMEM,
        everything_of(OWN + 2 * GHOST),
        name="wide",
        flops=10000000,
    )(pairs, state, wa, wb, totals)
    out = call(
        last_kernel,
        (f32(3, S, BLK),) * 3 + (f32(S, BLK),),
        [SMEM] + [VMEM] * 4,
        (VMEM,) * 4,
        [pltpu.VMEM((6, S, BLK), jnp.float32)] + everything_of(OWN + 2 * WIDE),
        name="last",
    )(pairs, state, la, lb, kept(totals))
    outs = [x.transpose(1, 0, 2)[None, None] for x in out[:3]]
    return (*outs, out[3][None, None])


def solution(mesh):
    five = P("len", "wid", None, None, None)
    four = P("len", "wid", None, None)
    three = P("len", "wid", None)
    in_specs = (five, five, five, four, three, four, four, four, three, three, P("len", "wid"))
    out_specs = (five, five, five, four)
    return jax.shard_map(body, mesh=mesh, in_specs=in_specs, out_specs=out_specs, check_vma=False)
```

```python
import functools
import math

import jax
import jax.numpy as jnp
from jax import lax
from jax.experimental import pallas as pl
from jax.experimental.pallas import tpu as pltpu
from jax.sharding import PartitionSpec as P

DENSITY = 1.9
TIME_STEP = 0.01
BLK = 128
S = 192
MOVE = 24
GHOST = 48
CORNER = 4
PAIRS = 128
BITS = 8
LBITS = 5
ROWS = 10
OWN = S
RECV = MOVE * BITS
WIDE = GHOST + 2 * CORNER
CORNERS = 2 * CORNER
G_LA, G_LB, G_WA, G_WB = 0, GHOST, 2 * GHOST, 2 * GHOST + WIDE
GBASE = OWN + RECV
T_SEND, T_FINAL, T_SIZE = 0, 192, 512
G_FACE, G_CORNER, G_SIZE = 0, 192, 256
C_CAT, C_START, C_END, C_SIZE = 0, 128, 144, 256
Q_A, Q_B, Q_SLOT, Q_END = 0, 136, 272, 408
Q_SIZE = 512
CAPS = {3: 32, 4: 40, 6: 24, 7: 24}
CATS = 12
SPARE = 11
MARGIN = 0.02
UNROLL = 3

SMEM = pl.BlockSpec(memory_space=pltpu.SMEM)
VMEM = pl.BlockSpec(memory_space=pltpu.VMEM)
HBM = pl.BlockSpec(memory_space=pltpu.HBM)
ANY = pl.BlockSpec(memory_space=pl.ANY)


def f32(*shape):
    return jax.ShapeDtypeStruct(shape, jnp.float32)


def ints(size):
    return jax.ShapeDtypeStruct((size,), jnp.int32)


def vmem(*shape):
    return pltpu.VMEM(shape, jnp.float32)


def call(body, out_shape, in_specs, out_specs, scratch=(), name=None, flops=0, aliases=None):
    return pl.pallas_call(
        body,
        out_shape=out_shape,
        in_specs=in_specs,
        out_specs=out_specs,
        scratch_shapes=list(scratch),
        name=name,
        input_output_aliases=aliases or {},
        compiler_params=pltpu.CompilerParams(vmem_limit_bytes=24 * 1024 * 1024),
        cost_estimate=pl.CostEstimate(flops=flops, transcendentals=0, bytes_accessed=1000000),
    )


def pack_kernel(slots_hbm, pos, vel, spin, rad, pool, send, slots, sems):
    copies = [
        pltpu.make_async_copy(slots_hbm, slots, sems.at[0]),
        pltpu.make_async_copy(pos, pool.at[0:3], sems.at[1]),
        pltpu.make_async_copy(vel, pool.at[3:6], sems.at[2]),
        pltpu.make_async_copy(spin, pool.at[6:9], sems.at[3]),
        pltpu.make_async_copy(rad, pool.at[9], sems.at[4]),
    ]
    for copy in copies:
        copy.start()
    for copy in copies:
        copy.wait()
    for j in range(MOVE):
        s = slots[0, j]
        for c in range(ROWS):
            send[c, j : j + 1, :] = pool[c, pl.ds(s, 1), :]


def table_kernel(counts, slots, tab):
    def init(i, _):
        for k in range(16):
            tab[T_FINAL + 16 * i + k] = 16 * i + k
        return 0

    lax.fori_loop(0, S // 16, init, 0)

    def move(t, _):
        live = counts[t]

        def one(i, _):
            first = 8 * i
            places = [slots[t, first + k] for k in range(8)]
            olds = [tab[T_FINAL + s] for s in places]
            for k in range(8):
                tab[T_SEND + MOVE * t + first + k] = olds[k]
            for k in range(8):
                j = first + k
                tab[T_FINAL + places[k]] = jnp.where(j < live, S + MOVE * t + j, olds[k])
            return 0

        lax.fori_loop(0, MOVE // 8, one, 0)
        return 0

    lax.fori_loop(0, BITS, move, 0)


def ghost_table_kernel(tab, ghosts, corners, out):
    for k in range(4):

        def face(i, _, k=k):
            values = [tab[T_FINAL + ghosts[k, 8 * i + g]] for g in range(8)]
            for g in range(8):
                out[G_FACE + GHOST * k + 8 * i + g] = values[g]
            return 0

        lax.fori_loop(0, GHOST // 8, face, 0)
        for g in range(CORNER):
            out[G_CORNER + CORNER * k + g] = tab[T_FINAL + corners[k, g]]


def count_kernel(tab, first, second, live_ref, out, start):
    live = live_ref[0, 0]
    for k in range(CATS):
        start[k] = 0

    def sort_in(i, _):
        cats = []
        for k in range(4):
            e = 4 * i + k
            b = second[e]
            code = jnp.maximum(tab[T_FINAL + first[e]], tab[T_FINAL + jnp.minimum(b, S - 1)])
            ready = jnp.where(code < S, 0, ((code - S) * 171 >> 12) + 1)
            g = b - S
            wide = (g >= GHOST) & (g < 3 * GHOST)
            where = jnp.where(b < S, ready, jnp.where(wide | (g >= 4 * GHOST), 10, 9))
            cats.append(jnp.where(e < live, where, SPARE))
        for k in range(4):
            out[C_CAT + 4 * i + k] = cats[k]
        for k in range(4):
            start[cats[k]] = start[cats[k]] + 1
        return 0

    lax.fori_loop(0, (live + 3) // 4, sort_in, 0)
    total = jnp.int32(0)
    done = jnp.int32(0)
    for k in range(CATS):
        out[C_START + k] = total
        total = total + start[k]
        if k < BITS:
            done = jnp.minimum(total, done + CAPS.get(k, 0))
            out[C_END + k] = done
        else:
            out[C_END + k] = total


def place_kernel(tab, cats, first, second, live_ref, out, start):
    live = live_ref[0, 0]
    even_w = odd("wid") == 0
    even_l = late() == 0
    for k in range(CATS):
        start[k] = cats[C_START + k]
        out[Q_END + k] = cats[C_END + k]

    def place(i, _):
        spots = []
        for k in range(4):
            e = 4 * i + k
            a = first[e]
            b = second[e]
            g = b - S
            h = g - 4 * GHOST
            diagonal = h >= 0
            face = jnp.where(g < GHOST, 0, jnp.where(g < 2 * GHOST, 1, jnp.where(g < 3 * GHOST, 2, 3)))
            wide = (face == 1) | (face == 2) | diagonal
            above = jnp.where(diagonal, (h & CORNER) == 0, face < 2)
            inside = GHOST + (h & (CORNER - 1)) + jnp.where(h < 2 * CORNER, 0, CORNER)
            inside = jnp.where(diagonal, inside, g - face * GHOST)
            wide_at = jnp.where(above == even_w, G_WA, G_WB) + inside
            long_at = jnp.where(above == even_l, G_LA, G_LB) + inside
            ghost = jnp.where(wide, wide_at, long_at) + GBASE
            own = tab[T_FINAL + jnp.minimum(b, S - 1)]
            spots.append((cats[C_CAT + e], a, tab[T_FINAL + a], jnp.where(b < S, own, ghost)))
        for where, a, near, far in spots:
            at = start[where]
            start[where] = at + 1
            out[Q_SLOT + at] = a
            out[Q_A + at] = near
            out[Q_B + at] = far
        return 0

    lax.fori_loop(0, (live + 3) // 4, place, 0)


def gather_rows(everything, tab, base, count, out, at):
    for j in range(count):
        s = tab[base + j]
        for c in range(ROWS):
            out[c, at + j : at + j + 1, :] = everything[c, pl.ds(s, 1), :]


def fill(everything, pool, received):
    everything[:, 0:OWN, :] = pool[...]
    for k, part in enumerate(received):
        everything[:, OWN + MOVE * k : OWN + MOVE * (k + 1), :] = part[...]


def step_kernel(t, tab, pool, *rest):
    received, send, everything = rest[:t], rest[-2], rest[-1]
    fill(everything, pool, received)
    gather_rows(everything, tab, T_SEND + MOVE * t, MOVE, send, 0)


def odd(axis):
    return lax.rem(lax.axis_index(axis), 2)


def late():
    return lax.rem(lax.axis_index("len") + lax.axis_index("wid"), 2)


def long_faces_kernel(tab, pool, *rest):
    la, lb, everything = rest[-3:]
    fill(everything, pool, rest[:BITS])
    up = 1 - late()
    for out, k in ((la, up), (lb, 1 - up)):
        gather_rows(everything, tab, G_FACE + 3 * GHOST * k, GHOST, out, 0)
        gather_rows(everything, tab, G_CORNER + 2 * CORNER * k, 2 * CORNER, out, GHOST)


def wide_faces_kernel(tab, pool, *rest):
    wa, wb, everything = rest[-3:]
    fill(everything, pool, rest[:BITS])
    up = 1 - odd("wid")
    for out, k in ((wa, up), (wb, 1 - up)):
        gather_rows(everything, tab, G_FACE + GHOST * (1 + k), GHOST, out, 0)


def forward_kernel(la, lb, _, wa_in, wb_in, wa, wb):
    up = 1 - odd("wid")
    flip = late()
    swap = jnp.full((CORNER, BLK), flip) == 1
    for out, k in ((wa, up), (wb, 1 - up)):
        for c in range(ROWS):
            at = pl.ds(GHOST + CORNER * k, CORNER)
            a, b = la[c, at, :], lb[c, at, :]
            out[c, GHOST : GHOST + CORNER, :] = jnp.where(swap, b, a)
            out[c, GHOST + CORNER : WIDE, :] = jnp.where(swap, a, b)


def rounded(x):
    return x.astype(jnp.bfloat16).astype(jnp.float32)


def factor(x, y, z, a, sub, near):
    pick = (sub & 1) == 0 if near else (sub & 2) == 0
    out = []
    for v in (jnp.where(sub < 4, x, y), jnp.where(sub < 4, z, a)):
        high = rounded(v)
        w = jnp.where(pick, high, v - high)
        out.append(w + w if near else w)
    c = a * a - ((x * x + y * y) + z * z)
    if near:
        c = c + MARGIN
    c1 = rounded(c)
    rest = c - c1
    c2 = rounded(rest)
    c3 = rest - c2
    b = 3 if near else 0
    ones = sub < 3 if near else (sub >= 3) & (sub < 6)
    tail = jnp.where(sub == b + 2, c3, jnp.where(ones, 1.0, 0.0))
    out.append(jnp.where(sub == b, c1, jnp.where(sub == b + 1, c2, tail)))
    out.append(jnp.zeros_like(x))
    return jnp.concatenate(out, axis=0).astype(jnp.bfloat16)


def contact(near, far, touching):
    px, py, pz, vx, vy, vz, sx, sy, sz, a = near
    qx, qy, qz, ux, uy, uz, tx, ty, tz, b = far
    rx, ry, rz = qx - px, qy - py, qz - pz
    d2 = (rx * rx + ry * ry) + (rz * rz + 0.01)
    inv = lax.rsqrt(d2)
    delta = jnp.maximum((a + b) - d2 * inv, 0.0)
    root = delta * lax.rsqrt(jnp.maximum(delta, 1e-30))
    nx, ny, nz = rx * inv, ry * inv, rz * inv
    wx, wy, wz = sx + tx, sy + ty, sz + tz
    dx, dy, dz = ux - vx, uy - vy, uz - vz
    ex = (dx - wy * nz) + wz * ny
    ey = (dy - wz * nx) + wx * nz
    ez = (dz - wx * ny) + wy * nx
    un = (ex * nx + ey * ny) + ez * nz
    g = jnp.where(touching, jnp.maximum(root * (30.0 * delta - un), 0.0), 0.0)
    gx, gy, gz = ex - un * nx, ey - un * ny, ez - un * nz
    c = g * lax.rsqrt((gx * gx + gy * gy) + (gz * gz + 0.01))
    cx, cy, cz = c * gx, c * gy, c * gz
    force = [cx, cy, cz, g * nx, g * ny, g * nz]
    return force + [ny * cz - nz * cy, nz * cx - nx * cz, nx * cy - ny * cx]


def eight_pairs(everything, nears, fars, used, near_s, far_s, words):
    sub = lax.broadcasted_iota(jnp.int32, (8, BLK), 0)

    def row(c, i):
        return jnp.broadcast_to(everything[c, pl.ds(i, 1), :], (8, BLK))

    for u in range(8):
        a, b = nears[u], fars[u]
        for c in range(ROWS):
            near_s[c, u : u + 1, :] = everything[c, pl.ds(a, 1), :]
            far_s[c, u : u + 1, :] = everything[c, pl.ds(b, 1), :]
        left = factor(*[row(c, b) for c in (0, 1, 2, 9)], sub, False)
        right = factor(*[row(c, a) for c in (0, 1, 2, 9)], sub, True)
        reach = lax.dot_general(
            left, right, (((0,), (0,)), ((), ())), preferred_element_type=jnp.float32
        )
        word = None
        for m in range(BLK // 8):
            bit = jnp.where(reach[8 * m : 8 * m + 8] > 0.0, 1 << m, 0)
            word = bit if word is None else word | bit
        word = word | (pltpu.roll(word, 4, 0) << 16)
        words[8 * u : 8 * u + 8, :] = word & used[u]
    left_over = [words[pl.ds(q, 8, stride=8), :] for q in range(4)]
    most = jnp.max(sum(lax.population_count(w) for w in left_over))

    def turned(x):
        return x[:6] + [x[6] * x[9], x[7] * x[9], x[8] * x[9], x[9]]

    near = turned([near_s[c] for c in range(ROWS)])
    far = turned([far_s[c] for c in range(ROWS)])

    def some(_, carry):
        w, acc = list(carry[:4]), list(carry[4:])
        for _ in range(UNROLL):
            some_in = [x != 0 for x in w[:3]]
            word = jnp.where(some_in[0], w[0], jnp.where(some_in[1], w[1], jnp.where(some_in[2], w[2], w[3])))
            q = jnp.where(some_in[0], 0, jnp.where(some_in[1], 1, jnp.where(some_in[2], 2, 3)))
            low = word & (-word)
            bit = 31 - lax.clz(low)
            w = [jnp.where(q == i, x ^ low, x) for i, x in enumerate(w)]
            j = (((bit & 15) << 3) + q + ((bit >> 4) << 2)) & (BLK - 1)
            terms = contact(near, [jnp.take_along_axis(x, j, axis=1) for x in far], low != 0)
            acc = [x + y for x, y in zip(acc, terms)]
        return (*w, *acc)

    zero = jnp.zeros((8, BLK), jnp.float32)
    passes = (most + UNROLL - 1) // UNROLL
    acc = lax.fori_loop(0, passes, some, (*left_over, *([zero] * 9)))[4:]
    force = [10.0 * acc[k] - 20.0 * acc[3 + k] for k in range(3)]
    scale = 10.0 * near[9]
    return force + [scale * acc[6 + k] for k in range(3)]


def all_pairs(everything, pairs, near_base, low, high, shift, scratch, sink):
    def group(i, _):
        at = [low + 8 * i + u for u in range(8)]
        inside = [jnp.minimum(e, high - 1) for e in at]
        used = [jnp.where(e < high, -1, 0) for e in at]
        nears = [pairs[near_base + e] for e in inside]
        fars = [pairs[Q_B + e] - shift for e in inside]
        sink(i, inside, eight_pairs(everything, nears, fars, used, *scratch))
        return 0

    lax.fori_loop(0, (high - low + 7) // 8, group, 0)


def early_kernel(t, pairs, pool, *rest):
    received, rows, everything, scratch = rest[:t], rest[t], rest[t + 1], rest[t + 2 :]
    low = pairs[Q_END + t - 1]
    high = pairs[Q_END + t]

    @pl.when(high > low)
    def _():
        fill(everything, pool, received)

        def sink(i, _, values):
            for k in range(6):
                rows[k, pl.ds(pl.multiple_of(8 * i, 8), 8), :] = values[k]

        all_pairs(everything, pairs, Q_A, low, high, 0, scratch, sink)


def into(totals, pairs):
    def sink(_, inside, values):
        for u in range(8):
            s = pairs[Q_SLOT + inside[u]]
            for k in range(6):
                totals[k, pl.ds(s, 1), :] = totals[k, pl.ds(s, 1), :] + values[k][u : u + 1]

    return sink


def middle_kernel(pairs, tab, pool, *rest):
    received = rest[:BITS]
    early = rest[BITS : BITS + len(CAPS)]
    state, totals, everything, *scratch = rest[BITS + len(CAPS) :]
    fill(everything, pool, received)

    def settle(i, _):
        for k in range(8):
            s = 8 * i + k
            at = tab[T_FINAL + s]
            for c in range(ROWS):
                state[c, pl.ds(s, 1), :] = everything[c, pl.ds(at, 1), :]
        return 0

    lax.fori_loop(0, S // 8, settle, 0)
    totals[...] = jnp.zeros((6, S, BLK), jnp.float32)
    for t, rows in zip(CAPS, early):
        low = pairs[Q_END + t - 1]
        high = pairs[Q_END + t]

        def add(e, _, low=low, rows=rows):
            s = pairs[Q_SLOT + e]
            for k in range(6):
                totals[k, pl.ds(s, 1), :] = totals[k, pl.ds(s, 1), :] + rows[k, pl.ds(e - low, 1), :]
            return 0

        lax.fori_loop(low, high, add, 0)
    low, high = pairs[Q_END + BITS - 1], pairs[Q_END + BITS]
    all_pairs(everything, pairs, Q_A, low, high, 0, scratch, into(totals, pairs))


def long_kernel(pairs, state, la, lb, totals_in, totals, everything, *scratch):
    totals[...] = totals_in[...]
    everything[:, 0:OWN, :] = state[...]
    everything[:, OWN : OWN + GHOST, :] = la[:, 0:GHOST, :]
    everything[:, OWN + GHOST : OWN + 2 * GHOST, :] = lb[:, 0:GHOST, :]
    low, high = pairs[Q_END + 8], pairs[Q_END + 9]
    all_pairs(everything, pairs, Q_SLOT, low, high, GBASE - OWN, scratch, into(totals, pairs))


def last_kernel(pairs, state, wa, wb, totals_in, pos, vel, spin, rad, totals, everything, *scratch):
    totals[...] = totals_in[...]
    everything[:, 0:OWN, :] = state[...]
    everything[:, OWN : OWN + WIDE, :] = wa[...]
    everything[:, OWN + WIDE : OWN + 2 * WIDE, :] = wb[...]
    low, high = pairs[Q_END + 9], pairs[Q_END + 10]
    shift = GBASE + G_WA - OWN
    all_pairs(everything, pairs, Q_SLOT, low, high, shift, scratch, into(totals, pairs))
    a = state[9]
    mass = (DENSITY * (4.0 / 3.0) * math.pi) * a * a * a
    inertia = 0.4 * mass * a * a
    by_mass = TIME_STEP / mass
    by_inertia = TIME_STEP / inertia
    for c in range(3):
        v = state[3 + c] + totals[c] * by_mass
        vel[c] = v
        pos[c] = state[c] + TIME_STEP * v
        spin[c] = state[6 + c] + totals[3 + c] * by_inertia
    rad[...] = a


def neighbours(size, low):
    pairs = [(i, i + 1) for i in range(low, size - 1, 2)]
    return pairs + [(j, i) for i, j in pairs]


def long_neighbours(n_len, n_wid, second):
    route = []
    for i in range(n_len):
        for w in range(n_wid):
            j = i + 1 if (i + w + second) % 2 == 0 else i - 1
            if 0 <= j < n_len:
                route.append((i * n_wid + w, j * n_wid + w))
    return route


def kept(x):
    return pltpu.with_memory_space_constraint(x, pltpu.VMEM)


def stays(x):
    return pltpu.with_memory_space_constraint(x, pltpu.HBM)


def everything_of(rows):
    work = [pltpu.VMEM((ROWS, 8, BLK), jnp.float32)] * 2 + [pltpu.VMEM((64, BLK), jnp.int32)]
    return [pltpu.VMEM((ROWS, rows, BLK), jnp.float32)] + work


def body(
    positions,
    velocities,
    spins,
    sphere_radii,
    swap_counts,
    swap_slots,
    ghost_slots,
    corner_slots,
    pair_first,
    pair_second,
    pair_live,
):
    n_len = lax.axis_size("len")
    n_wid = lax.axis_size("wid")
    planes = [stays(x[0, 0].transpose(1, 0, 2)) for x in (positions, velocities, spins)]
    slots = swap_slots[0, 0]
    pool_t, send_t = vmem(ROWS, S, BLK), vmem(ROWS, MOVE, BLK)
    pool, send = call(
        pack_kernel,
        (pool_t, send_t),
        [HBM] * 5,
        (VMEM, VMEM),
        [pltpu.SMEM((BITS, MOVE), jnp.int32), pltpu.SemaphoreType.DMA((5,))],
        name="pack",
    )(stays(slots), *planes, stays(sphere_radii[0, 0]))
    pool = kept(pool)
    lists = (pair_first[0, 0], pair_second[0, 0], pair_live)
    counter = [pltpu.SMEM((16,), jnp.int32)]
    tab = call(table_kernel, ints(T_SIZE), [SMEM] * 2, SMEM, name="tables", flops=2000000)(
        swap_counts[0, 0], slots
    )
    cats = call(count_kernel, ints(C_SIZE), [SMEM] * 4, SMEM, counter, "count", 2000000)(tab, *lists)
    pairs = call(place_kernel, ints(Q_SIZE), [SMEM] * 5, SMEM, counter, "place", 2000000)(
        tab, cats, *lists
    )
    gtab = call(ghost_table_kernel, ints(G_SIZE), [SMEM] * 3, SMEM, name="ghost_table", flops=1000000)(
        tab, ghost_slots[0, 0], corner_slots[0, 0]
    )
    windows = {1: [cats], 2: [pairs], 4: [gtab]}
    received, early = [], []
    behind = []
    for t in range(BITS):
        if t:
            send = call(
                functools.partial(step_kernel, t),
                send_t,
                [SMEM] + [VMEM] * (1 + t) + [ANY] * len(behind),
                VMEM,
                [pltpu.VMEM((ROWS, OWN + MOVE * t, BLK), jnp.float32)],
                name=f"step{t}",
            )(tab, pool, *received, *behind)
        axis, bit, size = ("len", t, n_len) if t < LBITS else ("wid", t - LBITS, n_wid)
        arrived = lax.ppermute(send, axis, [(i, i ^ (1 << bit)) for i in range(size)])
        behind = list(windows.get(t, []))
        if t in CAPS:
            rows = call(
                functools.partial(early_kernel, t),
                vmem(6, CAPS[t], BLK),
                [SMEM] + [VMEM] * (1 + t),
                VMEM,
                everything_of(OWN + MOVE * t),
                name=f"early{t}",
                flops=10000000,
            )(pairs, pool, *received)
            early.append(kept(rows))
            behind.append(early[-1])
        received.append(kept(arrived))
    wide_t = vmem(ROWS, WIDE, BLK)
    faces = [pltpu.VMEM((ROWS, OWN + RECV, BLK), jnp.float32)]
    la, lb = call(
        long_faces_kernel,
        (wide_t, wide_t),
        [SMEM] + [VMEM] * (1 + BITS) + [ANY] * len(behind),
        (VMEM, VMEM),
        faces,
        name="long_faces",
    )(gtab, pool, *received, *behind)
    sent = kept(la)
    la = kept(lax.ppermute(la, ("len", "wid"), long_neighbours(n_len, n_wid, 0)))
    lb = kept(lax.ppermute(lb, ("len", "wid"), long_neighbours(n_len, n_wid, 1)))
    wa, wb = call(
        wide_faces_kernel,
        (wide_t, wide_t),
        [SMEM] + [VMEM] * (1 + BITS) + [ANY],
        (VMEM, VMEM),
        faces,
        name="wide_faces",
        flops=1000000,
    )(gtab, pool, *received, sent)
    totals_t = vmem(6, S, BLK)
    state, totals = call(
        middle_kernel,
        (pool_t, totals_t),
        [SMEM] * 2 + [VMEM] * (1 + BITS + len(CAPS)),
        (VMEM, VMEM),
        everything_of(OWN + RECV),
        name="middle",
        flops=10000000,
    )(pairs, tab, pool, *received, *early)
    state, totals = kept(state), kept(totals)
    wa, wb = call(
        forward_kernel,
        (wide_t, wide_t),
        [VMEM] * 2 + [ANY] + [VMEM] * 2,
        (VMEM, VMEM),
        name="forward",
        aliases={3: 0, 4: 1},
    )(la, lb, totals, kept(wa), kept(wb))
    wa = kept(lax.ppermute(wa, "wid", neighbours(n_wid, 0)))
    wb = kept(lax.ppermute(wb, "wid", neighbours(n_wid, 1)))
    totals = call(
        long_kernel,
        totals_t,
        [SMEM] + [VMEM] * 4,
        VMEM,
        everything_of(OWN + 2 * GHOST),
        name="long",
        flops=10000000,
    )(pairs, state, la, lb, totals)
    out = call(
        last_kernel,
        (f32(3, S, BLK),) * 3 + (f32(S, BLK),),
        [SMEM] + [VMEM] * 4,
        (VMEM,) * 4,
        [pltpu.VMEM((6, S, BLK), jnp.float32)] + everything_of(OWN + 2 * WIDE),
        name="last",
    )(pairs, state, wa, wb, kept(totals))
    outs = [x.transpose(1, 0, 2)[None, None] for x in out[:3]]
    return (*outs, out[3][None, None])


def solution(mesh):
    five = P("len", "wid", None, None, None)
    four = P("len", "wid", None, None)
    three = P("len", "wid", None)
    in_specs = (five, five, five, four, three, four, four, four, three, three, P("len", "wid"))
    out_specs = (five, five, five, four)
    return jax.shard_map(body, mesh=mesh, in_specs=in_specs, out_specs=out_specs, check_vma=False)
```

```python
import functools
import math

import jax
import jax.numpy as jnp
from jax import lax
from jax.experimental import pallas as pl
from jax.experimental.pallas import tpu as pltpu
from jax.sharding import PartitionSpec as P

DENSITY = 1.9
TIME_STEP = 0.01
BLK = 128
S = 192
MOVE = 24
GHOST = 48
CORNER = 4
PAIRS = 128
BITS = 8
LBITS = 5
ROWS = 10
OWN = S
RECV = MOVE * BITS
WIDE = GHOST + 2 * CORNER
CORNERS = 2 * CORNER
G_LA, G_LB, G_WA, G_WB = 0, GHOST, 2 * GHOST, 2 * GHOST + WIDE
GBASE = OWN + RECV
T_SEND, T_FINAL, T_SIZE = 0, 192, 512
G_FACE, G_CORNER, G_SIZE = 0, 192, 256
C_CAT, C_START, C_END, C_SIZE = 0, 128, 144, 256
Q_A, Q_B, Q_SLOT, Q_END = 0, 136, 272, 408
Q_SIZE = 512
CAPS = {3: 32, 4: 40, 6: 24, 7: 24}
CATS = 12
SPARE = 11
MARGIN = 0.02
UNROLL = 3

SMEM = pl.BlockSpec(memory_space=pltpu.SMEM)
VMEM = pl.BlockSpec(memory_space=pltpu.VMEM)
HBM = pl.BlockSpec(memory_space=pltpu.HBM)
ANY = pl.BlockSpec(memory_space=pl.ANY)


def f32(*shape):
    return jax.ShapeDtypeStruct(shape, jnp.float32)


def ints(size):
    return jax.ShapeDtypeStruct((size,), jnp.int32)


def vmem(*shape):
    return pltpu.VMEM(shape, jnp.float32)


def call(body, out_shape, in_specs, out_specs, scratch=(), name=None, flops=0, aliases=None):
    return pl.pallas_call(
        body,
        out_shape=out_shape,
        in_specs=in_specs,
        out_specs=out_specs,
        scratch_shapes=list(scratch),
        name=name,
        input_output_aliases=aliases or {},
        compiler_params=pltpu.CompilerParams(vmem_limit_bytes=24 * 1024 * 1024),
        cost_estimate=pl.CostEstimate(flops=flops, transcendentals=0, bytes_accessed=1000000),
    )


def pack_kernel(slots_hbm, pos, vel, spin, rad, pool, send, slots, sems):
    copies = [
        pltpu.make_async_copy(slots_hbm, slots, sems.at[0]),
        pltpu.make_async_copy(pos, pool.at[0:3], sems.at[1]),
        pltpu.make_async_copy(vel, pool.at[3:6], sems.at[2]),
        pltpu.make_async_copy(spin, pool.at[6:9], sems.at[3]),
        pltpu.make_async_copy(rad, pool.at[9], sems.at[4]),
    ]
    for copy in copies:
        copy.start()
    for copy in copies:
        copy.wait()
    for j in range(MOVE):
        s = slots[0, j]
        for c in range(ROWS):
            send[c, j : j + 1, :] = pool[c, pl.ds(s, 1), :]


def table_kernel(counts, slots, tab):
    def init(i, _):
        for k in range(16):
            tab[T_FINAL + 16 * i + k] = 16 * i + k
        return 0

    lax.fori_loop(0, S // 16, init, 0)

    def move(t, _):
        live = counts[t]

        def one(i, _):
            first = 8 * i
            places = [slots[t, first + k] for k in range(8)]
            olds = [tab[T_FINAL + s] for s in places]
            for k in range(8):
                tab[T_SEND + MOVE * t + first + k] = olds[k]
            for k in range(8):
                j = first + k
                tab[T_FINAL + places[k]] = jnp.where(j < live, S + MOVE * t + j, olds[k])
            return 0

        lax.fori_loop(0, MOVE // 8, one, 0)
        return 0

    lax.fori_loop(0, BITS, move, 0)


def ghost_table_kernel(tab, ghosts, corners, out):
    for k in range(4):

        def face(i, _, k=k):
            values = [tab[T_FINAL + ghosts[k, 8 * i + g]] for g in range(8)]
            for g in range(8):
                out[G_FACE + GHOST * k + 8 * i + g] = values[g]
            return 0

        lax.fori_loop(0, GHOST // 8, face, 0)
        for g in range(CORNER):
            out[G_CORNER + CORNER * k + g] = tab[T_FINAL + corners[k, g]]


def count_kernel(tab, first, second, live_ref, out, start):
    live = live_ref[0, 0]
    for k in range(CATS):
        start[k] = 0

    def sort_in(i, _):
        cats = []
        for k in range(4):
            e = 4 * i + k
            b = second[e]
            code = jnp.maximum(tab[T_FINAL + first[e]], tab[T_FINAL + jnp.minimum(b, S - 1)])
            ready = jnp.where(code < S, 0, ((code - S) * 171 >> 12) + 1)
            g = b - S
            wide = (g >= GHOST) & (g < 3 * GHOST)
            where = jnp.where(b < S, ready, jnp.where(wide | (g >= 4 * GHOST), 10, 9))
            cats.append(jnp.where(e < live, where, SPARE))
        for k in range(4):
            out[C_CAT + 4 * i + k] = cats[k]
        for k in range(4):
            start[cats[k]] = start[cats[k]] + 1
        return 0

    lax.fori_loop(0, (live + 3) // 4, sort_in, 0)
    total = jnp.int32(0)
    done = jnp.int32(0)
    for k in range(CATS):
        out[C_START + k] = total
        total = total + start[k]
        if k < BITS:
            done = jnp.minimum(total, done + CAPS.get(k, 0))
            out[C_END + k] = done
        else:
            out[C_END + k] = total


def place_kernel(tab, cats, first, second, live_ref, out, start):
    live = live_ref[0, 0]
    even_w = odd("wid") == 0
    even_l = late() == 0
    for k in range(CATS):
        start[k] = cats[C_START + k]
        out[Q_END + k] = cats[C_END + k]

    def place(i, _):
        spots = []
        for k in range(4):
            e = 4 * i + k
            a = first[e]
            b = second[e]
            g = b - S
            h = g - 4 * GHOST
            diagonal = h >= 0
            face = jnp.where(g < GHOST, 0, jnp.where(g < 2 * GHOST, 1, jnp.where(g < 3 * GHOST, 2, 3)))
            wide = (face == 1) | (face == 2) | diagonal
            above = jnp.where(diagonal, (h & CORNER) == 0, face < 2)
            inside = GHOST + (h & (CORNER - 1)) + jnp.where(h < 2 * CORNER, 0, CORNER)
            inside = jnp.where(diagonal, inside, g - face * GHOST)
            wide_at = jnp.where(above == even_w, G_WA, G_WB) + inside
            long_at = jnp.where(above == even_l, G_LA, G_LB) + inside
            ghost = jnp.where(wide, wide_at, long_at) + GBASE
            own = tab[T_FINAL + jnp.minimum(b, S - 1)]
            spots.append((cats[C_CAT + e], a, tab[T_FINAL + a], jnp.where(b < S, own, ghost)))
        for where, a, near, far in spots:
            at = start[where]
            start[where] = at + 1
            out[Q_SLOT + at] = a
            out[Q_A + at] = near
            out[Q_B + at] = far
        return 0

    lax.fori_loop(0, (live + 3) // 4, place, 0)


def gather_rows(everything, tab, base, count, out, at):
    for j in range(count):
        s = tab[base + j]
        for c in range(ROWS):
            out[c, at + j : at + j + 1, :] = everything[c, pl.ds(s, 1), :]


def fill(everything, pool, received):
    everything[:, 0:OWN, :] = pool[...]
    for k, part in enumerate(received):
        everything[:, OWN + MOVE * k : OWN + MOVE * (k + 1), :] = part[...]


def step_kernel(t, tab, pool, *rest):
    received, send, everything = rest[:t], rest[-2], rest[-1]
    fill(everything, pool, received)
    gather_rows(everything, tab, T_SEND + MOVE * t, MOVE, send, 0)


def odd(axis):
    return lax.rem(lax.axis_index(axis), 2)


def late():
    return lax.rem(lax.axis_index("len") + lax.axis_index("wid"), 2)


def long_faces_kernel(tab, pool, *rest):
    la, lb, everything = rest[-3:]
    fill(everything, pool, rest[:BITS])
    up = 1 - late()
    for out, k in ((la, up), (lb, 1 - up)):
        gather_rows(everything, tab, G_FACE + 3 * GHOST * k, GHOST, out, 0)
        gather_rows(everything, tab, G_CORNER + 2 * CORNER * k, 2 * CORNER, out, GHOST)


def wide_faces_kernel(tab, pool, *rest):
    wa, wb, everything = rest[-3:]
    fill(everything, pool, rest[:BITS])
    up = 1 - odd("wid")
    for out, k in ((wa, up), (wb, 1 - up)):
        gather_rows(everything, tab, G_FACE + GHOST * (1 + k), GHOST, out, 0)


def forward_kernel(la, lb, _, wa_in, wb_in, wa, wb):
    up = 1 - odd("wid")
    flip = late()
    swap = jnp.full((CORNER, BLK), flip) == 1
    for out, k in ((wa, up), (wb, 1 - up)):
        for c in range(ROWS):
            at = pl.ds(GHOST + CORNER * k, CORNER)
            a, b = la[c, at, :], lb[c, at, :]
            out[c, GHOST : GHOST + CORNER, :] = jnp.where(swap, b, a)
            out[c, GHOST + CORNER : WIDE, :] = jnp.where(swap, a, b)


def rounded(x):
    return x.astype(jnp.bfloat16).astype(jnp.float32)


def factor(x, y, z, a, sub, near):
    pick = (sub & 1) == 0 if near else (sub & 2) == 0
    out = []
    for v in (jnp.where(sub < 4, x, y), jnp.where(sub < 4, z, a)):
        high = rounded(v)
        w = jnp.where(pick, high, v - high)
        out.append(w + w if near else w)
    c = a * a - ((x * x + y * y) + z * z)
    if near:
        c = c + MARGIN
    c1 = rounded(c)
    rest = c - c1
    c2 = rounded(rest)
    c3 = rest - c2
    b = 3 if near else 0
    ones = sub < 3 if near else (sub >= 3) & (sub < 6)
    tail = jnp.where(sub == b + 2, c3, jnp.where(ones, 1.0, 0.0))
    out.append(jnp.where(sub == b, c1, jnp.where(sub == b + 1, c2, tail)))
    out.append(jnp.zeros_like(x))
    return jnp.concatenate(out, axis=0).astype(jnp.bfloat16)


def contact(near, far, touching):
    px, py, pz, vx, vy, vz, sx, sy, sz, a = near
    qx, qy, qz, ux, uy, uz, tx, ty, tz, b = far
    rx, ry, rz = qx - px, qy - py, qz - pz
    d2 = (rx * rx + ry * ry) + (rz * rz + 0.01)
    inv = lax.rsqrt(d2)
    delta = jnp.maximum((a + b) - d2 * inv, 0.0)
    root = delta * lax.rsqrt(jnp.maximum(delta, 1e-30))
    nx, ny, nz = rx * inv, ry * inv, rz * inv
    wx, wy, wz = sx + tx, sy + ty, sz + tz
    dx, dy, dz = ux - vx, uy - vy, uz - vz
    ex = (dx - wy * nz) + wz * ny
    ey = (dy - wz * nx) + wx * nz
    ez = (dz - wx * ny) + wy * nx
    un = (ex * nx + ey * ny) + ez * nz
    g = jnp.where(touching, jnp.maximum(root * (30.0 * delta - un), 0.0), 0.0)
    gx, gy, gz = ex - un * nx, ey - un * ny, ez - un * nz
    c = g * lax.rsqrt((gx * gx + gy * gy) + (gz * gz + 0.01))
    cx, cy, cz = c * gx, c * gy, c * gz
    force = [cx, cy, cz, g * nx, g * ny, g * nz]
    return force + [ny * cz - nz * cy, nz * cx - nx * cz, nx * cy - ny * cx]


def eight_pairs(own, everything, nears, fars, used, near_s, far_s, words):
    sub = lax.broadcasted_iota(jnp.int32, (8, BLK), 0)

    def row(source, c, i):
        return jnp.broadcast_to(source[c, pl.ds(i, 1), :], (8, BLK))

    for u in range(8):
        a, b = nears[u], fars[u]
        for c in range(ROWS):
            near_s[c, u : u + 1, :] = own[c, pl.ds(a, 1), :]
            far_s[c, u : u + 1, :] = everything[c, pl.ds(b, 1), :]
        left = factor(*[row(everything, c, b) for c in (0, 1, 2, 9)], sub, False)
        right = factor(*[row(own, c, a) for c in (0, 1, 2, 9)], sub, True)
        reach = lax.dot_general(
            left, right, (((0,), (0,)), ((), ())), preferred_element_type=jnp.float32
        )
        word = None
        for m in range(BLK // 8):
            bit = jnp.where(reach[8 * m : 8 * m + 8] > 0.0, 1 << m, 0)
            word = bit if word is None else word | bit
        word = word | (pltpu.roll(word, 4, 0) << 16)
        words[8 * u : 8 * u + 8, :] = word & used[u]
    left_over = [words[pl.ds(q, 8, stride=8), :] for q in range(4)]
    most = jnp.max(sum(lax.population_count(w) for w in left_over))

    def turned(x):
        return x[:6] + [x[6] * x[9], x[7] * x[9], x[8] * x[9], x[9]]

    near = turned([near_s[c] for c in range(ROWS)])
    far = turned([far_s[c] for c in range(ROWS)])

    def some(_, carry):
        w, acc = list(carry[:4]), list(carry[4:])
        for _ in range(UNROLL):
            some_in = [x != 0 for x in w[:3]]
            word = jnp.where(some_in[0], w[0], jnp.where(some_in[1], w[1], jnp.where(some_in[2], w[2], w[3])))
            q = jnp.where(some_in[0], 0, jnp.where(some_in[1], 1, jnp.where(some_in[2], 2, 3)))
            low = word & (-word)
            bit = 31 - lax.clz(low)
            w = [jnp.where(q == i, x ^ low, x) for i, x in enumerate(w)]
            j = (((bit & 15) << 3) + q + ((bit >> 4) << 2)) & (BLK - 1)
            terms = contact(near, [jnp.take_along_axis(x, j, axis=1) for x in far], low != 0)
            acc = [x + y for x, y in zip(acc, terms)]
        return (*w, *acc)

    zero = jnp.zeros((8, BLK), jnp.float32)
    passes = (most + UNROLL - 1) // UNROLL
    acc = lax.fori_loop(0, passes, some, (*left_over, *([zero] * 9)))[4:]
    force = [10.0 * acc[k] - 20.0 * acc[3 + k] for k in range(3)]
    scale = 10.0 * near[9]
    return force + [scale * acc[6 + k] for k in range(3)]


def all_pairs(own, everything, pairs, near_base, low, high, shift, scratch, sink):
    def group(i, _):
        at = [low + 8 * i + u for u in range(8)]
        inside = [jnp.minimum(e, high - 1) for e in at]
        used = [jnp.where(e < high, -1, 0) for e in at]
        nears = [pairs[near_base + e] for e in inside]
        fars = [pairs[Q_B + e] - shift for e in inside]
        sink(i, inside, eight_pairs(own, everything, nears, fars, used, *scratch))
        return 0

    lax.fori_loop(0, (high - low + 7) // 8, group, 0)


def early_kernel(t, pairs, pool, *rest):
    received, rows, everything, scratch = rest[:t], rest[t], rest[t + 1], rest[t + 2 :]
    low = pairs[Q_END + t - 1]
    high = pairs[Q_END + t]

    @pl.when(high > low)
    def _():
        fill(everything, pool, received)

        def sink(i, _, values):
            for k in range(6):
                rows[k, pl.ds(pl.multiple_of(8 * i, 8), 8), :] = values[k]

        all_pairs(everything, everything, pairs, Q_A, low, high, 0, scratch, sink)


def into(totals, pairs):
    def sink(_, inside, values):
        for u in range(8):
            s = pairs[Q_SLOT + inside[u]]
            for k in range(6):
                totals[k, pl.ds(s, 1), :] = totals[k, pl.ds(s, 1), :] + values[k][u : u + 1]

    return sink


def middle_kernel(pairs, tab, pool, *rest):
    received = rest[:BITS]
    early = rest[BITS : BITS + len(CAPS)]
    state, totals, everything, *scratch = rest[BITS + len(CAPS) :]
    fill(everything, pool, received)

    def settle(i, _):
        for k in range(8):
            s = 8 * i + k
            at = tab[T_FINAL + s]
            for c in range(ROWS):
                state[c, pl.ds(s, 1), :] = everything[c, pl.ds(at, 1), :]
        return 0

    lax.fori_loop(0, S // 8, settle, 0)
    totals[...] = jnp.zeros((6, S, BLK), jnp.float32)
    for t, rows in zip(CAPS, early):
        low = pairs[Q_END + t - 1]
        high = pairs[Q_END + t]

        def add(e, _, low=low, rows=rows):
            s = pairs[Q_SLOT + e]
            for k in range(6):
                totals[k, pl.ds(s, 1), :] = totals[k, pl.ds(s, 1), :] + rows[k, pl.ds(e - low, 1), :]
            return 0

        lax.fori_loop(low, high, add, 0)
    low, high = pairs[Q_END + BITS - 1], pairs[Q_END + BITS]
    all_pairs(everything, everything, pairs, Q_A, low, high, 0, scratch, into(totals, pairs))


def long_kernel(pairs, state, la, lb, totals_in, totals, everything, *scratch):
    totals[...] = totals_in[...]
    everything[:, 0:GHOST, :] = la[:, 0:GHOST, :]
    everything[:, GHOST : 2 * GHOST, :] = lb[:, 0:GHOST, :]
    low, high = pairs[Q_END + 8], pairs[Q_END + 9]
    all_pairs(state, everything, pairs, Q_SLOT, low, high, GBASE, scratch, into(totals, pairs))


def last_kernel(pairs, state, wa, wb, totals_in, pos, vel, spin, rad, totals, everything, *scratch):
    totals[...] = totals_in[...]
    everything[:, 0:WIDE, :] = wa[...]
    everything[:, WIDE : 2 * WIDE, :] = wb[...]
    low, high = pairs[Q_END + 9], pairs[Q_END + 10]
    shift = GBASE + G_WA
    all_pairs(state, everything, pairs, Q_SLOT, low, high, shift, scratch, into(totals, pairs))
    a = state[9]
    mass = (DENSITY * (4.0 / 3.0) * math.pi) * a * a * a
    inertia = 0.4 * mass * a * a
    by_mass = TIME_STEP / mass
    by_inertia = TIME_STEP / inertia
    for c in range(3):
        v = state[3 + c] + totals[c] * by_mass
        vel[c] = v
        pos[c] = state[c] + TIME_STEP * v
        spin[c] = state[6 + c] + totals[3 + c] * by_inertia
    rad[...] = a


def neighbours(size, low):
    pairs = [(i, i + 1) for i in range(low, size - 1, 2)]
    return pairs + [(j, i) for i, j in pairs]


def long_neighbours(n_len, n_wid, second):
    route = []
    for i in range(n_len):
        for w in range(n_wid):
            j = i + 1 if (i + w + second) % 2 == 0 else i - 1
            if 0 <= j < n_len:
                route.append((i * n_wid + w, j * n_wid + w))
    return route


def kept(x):
    return pltpu.with_memory_space_constraint(x, pltpu.VMEM)


def stays(x):
    return pltpu.with_memory_space_constraint(x, pltpu.HBM)


def everything_of(rows):
    work = [pltpu.VMEM((ROWS, 8, BLK), jnp.float32)] * 2 + [pltpu.VMEM((64, BLK), jnp.int32)]
    return [pltpu.VMEM((ROWS, rows, BLK), jnp.float32)] + work


def body(
    positions,
    velocities,
    spins,
    sphere_radii,
    swap_counts,
    swap_slots,
    ghost_slots,
    corner_slots,
    pair_first,
    pair_second,
    pair_live,
):
    n_len = lax.axis_size("len")
    n_wid = lax.axis_size("wid")
    planes = [stays(x[0, 0].transpose(1, 0, 2)) for x in (positions, velocities, spins)]
    slots = swap_slots[0, 0]
    pool_t, send_t = vmem(ROWS, S, BLK), vmem(ROWS, MOVE, BLK)
    pool, send = call(
        pack_kernel,
        (pool_t, send_t),
        [HBM] * 5,
        (VMEM, VMEM),
        [pltpu.SMEM((BITS, MOVE), jnp.int32), pltpu.SemaphoreType.DMA((5,))],
        name="pack",
    )(stays(slots), *planes, stays(sphere_radii[0, 0]))
    pool = kept(pool)
    lists = (pair_first[0, 0], pair_second[0, 0], pair_live)
    counter = [pltpu.SMEM((16,), jnp.int32)]
    tab = call(table_kernel, ints(T_SIZE), [SMEM] * 2, SMEM, name="tables", flops=2000000)(
        swap_counts[0, 0], slots
    )
    cats = call(count_kernel, ints(C_SIZE), [SMEM] * 4, SMEM, counter, "count", 2000000)(tab, *lists)
    pairs = call(place_kernel, ints(Q_SIZE), [SMEM] * 5, SMEM, counter, "place", 2000000)(
        tab, cats, *lists
    )
    gtab = call(ghost_table_kernel, ints(G_SIZE), [SMEM] * 3, SMEM, name="ghost_table", flops=1000000)(
        tab, ghost_slots[0, 0], corner_slots[0, 0]
    )
    windows = {1: [cats], 2: [pairs], 4: [gtab]}
    received, early = [], []
    behind = []
    for t in range(BITS):
        if t:
            send = call(
                functools.partial(step_kernel, t),
                send_t,
                [SMEM] + [VMEM] * (1 + t) + [ANY] * len(behind),
                VMEM,
                [pltpu.VMEM((ROWS, OWN + MOVE * t, BLK), jnp.float32)],
                name=f"step{t}",
            )(tab, pool, *received, *behind)
        axis, bit, size = ("len", t, n_len) if t < LBITS else ("wid", t - LBITS, n_wid)
        arrived = lax.ppermute(send, axis, [(i, i ^ (1 << bit)) for i in range(size)])
        behind = list(windows.get(t, []))
        if t in CAPS:
            rows = call(
                functools.partial(early_kernel, t),
                vmem(6, CAPS[t], BLK),
                [SMEM] + [VMEM] * (1 + t),
                VMEM,
                everything_of(OWN + MOVE * t),
                name=f"early{t}",
                flops=10000000,
            )(pairs, pool, *received)
            early.append(kept(rows))
            behind.append(early[-1])
        received.append(kept(arrived))
    wide_t = vmem(ROWS, WIDE, BLK)
    faces = [pltpu.VMEM((ROWS, OWN + RECV, BLK), jnp.float32)]
    la, lb = call(
        long_faces_kernel,
        (wide_t, wide_t),
        [SMEM] + [VMEM] * (1 + BITS) + [ANY] * len(behind),
        (VMEM, VMEM),
        faces,
        name="long_faces",
    )(gtab, pool, *received, *behind)
    sent = kept(la)
    la = kept(lax.ppermute(la, ("len", "wid"), long_neighbours(n_len, n_wid, 0)))
    lb = kept(lax.ppermute(lb, ("len", "wid"), long_neighbours(n_len, n_wid, 1)))
    wa, wb = call(
        wide_faces_kernel,
        (wide_t, wide_t),
        [SMEM] + [VMEM] * (1 + BITS) + [ANY],
        (VMEM, VMEM),
        faces,
        name="wide_faces",
        flops=1000000,
    )(gtab, pool, *received, sent)
    totals_t = vmem(6, S, BLK)
    state, totals = call(
        middle_kernel,
        (pool_t, totals_t),
        [SMEM] * 2 + [VMEM] * (1 + BITS + len(CAPS)),
        (VMEM, VMEM),
        everything_of(OWN + RECV),
        name="middle",
        flops=10000000,
    )(pairs, tab, pool, *received, *early)
    state, totals = kept(state), kept(totals)
    wa, wb = call(
        forward_kernel,
        (wide_t, wide_t),
        [VMEM] * 2 + [ANY] + [VMEM] * 2,
        (VMEM, VMEM),
        name="forward",
        aliases={3: 0, 4: 1},
    )(la, lb, totals, kept(wa), kept(wb))
    wa = kept(lax.ppermute(wa, "wid", neighbours(n_wid, 0)))
    wb = kept(lax.ppermute(wb, "wid", neighbours(n_wid, 1)))
    totals = call(
        long_kernel,
        totals_t,
        [SMEM] + [VMEM] * 4,
        VMEM,
        everything_of(2 * GHOST),
        name="long",
        flops=10000000,
    )(pairs, state, la, lb, totals)
    out = call(
        last_kernel,
        (f32(3, S, BLK),) * 3 + (f32(S, BLK),),
        [SMEM] + [VMEM] * 4,
        (VMEM,) * 4,
        [pltpu.VMEM((6, S, BLK), jnp.float32)] + everything_of(2 * WIDE),
        name="last",
    )(pairs, state, wa, wb, kept(totals))
    outs = [x.transpose(1, 0, 2)[None, None] for x in out[:3]]
    return (*outs, out[3][None, None])


def solution(mesh):
    five = P("len", "wid", None, None, None)
    four = P("len", "wid", None, None)
    three = P("len", "wid", None)
    in_specs = (five, five, five, four, three, four, four, four, three, three, P("len", "wid"))
    out_specs = (five, five, five, four)
    return jax.shard_map(body, mesh=mesh, in_specs=in_specs, out_specs=out_specs, check_vma=False)
```
